512 devices in a mesh: blk: 8 (over y_lo, x), dom: 64 (over y_hi, z, core).
Axes of the slice: x: 4, y: 8 (y_hi: 4, y_lo: 2; y = y_hi * 2 + y_lo), z: 8, core: 2. Of those that a mesh axis runs over, the one named last changes fastest.
Arguments:
- node_feat: bfloat16 [131072, 256], P(('blk', 'dom')), may hold values from -6 to 6
- cotangent: bfloat16 [131072, 256], P(('blk', 'dom')), may hold values from -6 to 6
- self_weight: bfloat16 [256, 256], replicated, may hold values from -0.375 to 0.375
- neigh_weight: bfloat16 [256, 256], replicated, may hold values from -0.375 to 0.375
- tile_weights: bfloat16 [512, 8, 4, 128, 128], P(('blk', 'dom')), as said below
- tile_dest: int32 [512, 8, 4], P(('blk', 'dom')), may hold values from 0 to 2, as said below
- tile_source: int32 [512, 8, 4], P(('blk', 'dom')), may hold values from 0 to 1
- hub_weights: bfloat16 [512, 64, 32, 128], P(('blk', 'dom')), as said below
- hub_source: int32 [512, 64], P(('blk', 'dom')), may hold values from 0 to 1
- hub_slots: int32 [512, 64, 32], P(('blk', 'dom')), may hold values from 0 to 256, as said below
Outputs:
- layer_out: bfloat16 [131072, 256], P(('blk', 'dom'))
- feat_grad: bfloat16 [131072, 256], P(('blk', 'dom'))
- self_grad: float32 [256, 256], replicated
- neigh_grad: float32 [256, 256], replicated
The draws below stay inside these ranges and needn't reach their ends.
Inputs may be any that keep to these rules, and one draw needn't show every extreme that they name: `tile_weights`: nonnegative edge weights, zero where there is no edge. `hub_weights`: nonnegative edge weights, zero where there is no edge. `tile_dest`: 2 marks an empty slot; in the slots of one range for one panel the filled ones come first. `hub_slots`: 256 marks a padded slot; rows may repeat.
All inputs are finite; a program needn't handle non-finite values.
Results may differ from the reference program's by a relative error of at most 0.019.
Values may be sent and summed in bfloat16 or wider, within the bound.
No kernel may reach another device: no remote copies, remote signals or barrier semaphores. Data moves between devices by JAX's collectives and lax.ppermute only.
A program may use at most 64 MiB of HBM per device.

```python
import math
import jax
import jax.numpy as jnp
from jax import lax

WIDTH = 256
TILE = 128
HUB_ROWS = 32
BLOCKS_DEV = 2
SLOTS = 4
ROWS = 256
SHARDS = 512
NODES = 131072
N_BLK = 8
N_DOM = 64


def edge_values(key, shape):
    key_mag, key_keep = jax.random.split(key, 2)
    magnitude = jnp.exp(jax.random.uniform(key_mag, shape, jnp.float32, math.log(0.25), math.log(4.0)))
    keep = jax.random.bernoulli(key_keep, 0.5, shape)
    values = jnp.where(keep, magnitude, 0.0)
    return values.astype(jnp.bfloat16)


def draw_tile_weights(key, part):
    return edge_values(jax.random.fold_in(key, 11), (SHARDS, N_BLK, SLOTS, TILE, TILE))


def draw_hub_weights(key, part):
    return edge_values(jax.random.fold_in(key, 23), (SHARDS, N_DOM, HUB_ROWS, TILE))


def draw_tile_dest(key, part):
    key_live, key_full, key_block = jax.random.split(jax.random.fold_in(key, 37), 3)
    live = jax.random.randint(key_live, (SHARDS, N_BLK, 1), 0, SLOTS + 1)
    full = jax.random.randint(key_full, (SHARDS, 1, 1), 0, N_BLK)
    panel = jnp.arange(N_BLK, dtype=jnp.int32)[None, :, None]
    live = jnp.where(panel == full, SLOTS, live)
    live = jnp.where(panel == (full + 1) % N_BLK, SLOTS - 1, live)
    blocks = jax.random.randint(key_block, (SHARDS, N_BLK, SLOTS), 0, BLOCKS_DEV)
    slot = jnp.arange(SLOTS, dtype=jnp.int32)[None, None, :]
    return jnp.where(slot < live, blocks, BLOCKS_DEV).astype(jnp.int32)


def draw_hub_slots(key, part):
    key_rows, key_place = jax.random.split(jax.random.fold_in(key, 41), 2)
    values = jax.random.randint(key_rows, (SHARDS, N_DOM * HUB_ROWS), 0, ROWS + ROWS // 4)
    values = jnp.minimum(values, ROWS)
    place = jax.random.randint(key_place, (SHARDS, 1), 0, N_DOM * HUB_ROWS)
    spots = jnp.arange(N_DOM * HUB_ROWS, dtype=jnp.int32)[None, :]
    values = jnp.where(spots == place, ROWS, values)
    return values.reshape(SHARDS, N_DOM, HUB_ROWS).astype(jnp.int32)


def plant(drawn, rng, smallest, top_value):
    spot = [jax.random.randint(jax.random.fold_in(rng, axis), (), 0, length) for axis, length in enumerate(drawn.shape)]
    longest = drawn.shape.index(max(drawn.shape))
    next_to = spot[:longest] + [(spot[longest] + 1) % drawn.shape[longest]] + spot[longest + 1:]
    return drawn.at[tuple(spot)].set(smallest).at[tuple(next_to)].set(top_value)


def block_levels(own_key, dims, cuts, least, largest):
    gain = 1.0
    for position, shards_of in cuts:
        heights = jax.random.uniform(jax.random.fold_in(jax.random.fold_in(own_key, 6), position), (shards_of,), jnp.float32, least / len(cuts), largest / len(cuts))
        gain = gain * jnp.repeat(jnp.exp(heights), dims[position] // shards_of).reshape((-1,) + (1,) * (len(dims) - 1 - position))
    return gain


def noise(key, dims, width, reach, cuts=(), kind=jnp.bfloat16):
    factor_of = block_levels(key, dims, cuts, -0.22, 0.18) if cuts else 1.0
    drawn = jax.random.normal(key, dims, jnp.float32) * width * factor_of
    return jnp.minimum(jnp.maximum(drawn, -reach), reach).astype(kind)


def setup_inputs(seed: int = 0) -> dict:
    key_of = jax.random.split(jax.random.key(seed), 11)
    return {
        "node_feat": noise(key_of[0], (NODES, WIDTH), 1.0, 6.0, ((0, 512),)),
        "cotangent": noise(key_of[1], (NODES, WIDTH), 1.0, 6.0, ((0, 512),)),
        "self_weight": noise(key_of[2], (WIDTH, WIDTH), WIDTH ** -0.5, 0.375),
        "neigh_weight": noise(key_of[3], (WIDTH, WIDTH), WIDTH ** -0.5, 0.375),
        "tile_weights": draw_tile_weights(jax.random.fold_in(key_of[10], 71), 0),
        "tile_dest": draw_tile_dest(jax.random.fold_in(key_of[10], 71), 0),
        "tile_source": plant(jax.random.randint(key_of[6], (SHARDS, N_BLK, SLOTS), 0, BLOCKS_DEV), jax.random.fold_in(key_of[6], 1), 0, BLOCKS_DEV - 1).astype(jnp.int32),
        "hub_weights": draw_hub_weights(jax.random.fold_in(key_of[10], 71), 0),
        "hub_source": plant(jax.random.randint(key_of[8], (SHARDS, N_DOM), 0, BLOCKS_DEV), jax.random.fold_in(key_of[8], 1), 0, BLOCKS_DEV - 1).astype(jnp.int32),
        "hub_slots": draw_hub_slots(jax.random.fold_in(key_of[10], 71), 0),
    }


def hub_targets(hub_slots, index):
    blk_id = index // N_DOM
    dom_id = index % N_DOM
    owners = (blk_id * N_DOM + jnp.arange(N_DOM, dtype=jnp.int32)).astype(jnp.int32)
    slots = hub_slots[owners, dom_id]
    return jnp.where(slots == ROWS, NODES, owners[:, None] * ROWS + slots).astype(jnp.int32)

def reference(node_feat, cotangent, self_weight, neigh_weight, tile_weights, tile_dest, tile_source, hub_weights, hub_source, hub_slots):
    feat = node_feat.reshape(N_BLK, N_DOM, BLOCKS_DEV, TILE, WIDTH)
    lanes = jnp.arange(N_BLK, dtype=jnp.int32)[:, None]

    def local_forward(index):
        dom_id = index % N_DOM
        tiles = tile_weights[index].astype(jnp.float32)
        panels = lax.dynamic_index_in_dim(feat, dom_id, 1, False)
        blocks = panels[lanes, tile_source[index]].astype(jnp.float32)
        contrib = jnp.einsum('qkrc,qkcf->qkrf', tiles, blocks)
        placing = jax.nn.one_hot(tile_dest[index], BLOCKS_DEV, dtype=jnp.float32)
        summed = jnp.einsum('qkn,qkrf->nrf', placing, contrib)
        degree = jnp.einsum('qkn,qkr->nr', placing, lax.optimization_barrier(jnp.sum(tiles, axis=-1)))
        return (summed.reshape(ROWS, WIDTH), degree.reshape(ROWS))
    indices = jnp.arange(SHARDS, dtype=jnp.int32)
    summed, degree = lax.map(local_forward, indices)
    summed = summed.reshape(NODES, WIDTH)
    degree = degree.reshape(NODES)
    flat_blocks = node_feat.reshape(SHARDS, BLOCKS_DEV, TILE, WIDTH)

    def hub_forward(index, carry):
        index = jnp.asarray(index).astype(jnp.int32)
        total, weight = carry
        hub_tiles = hub_weights[index].astype(jnp.float32)
        blocks = flat_blocks[index][hub_source[index]].astype(jnp.float32)
        part = jnp.einsum('ohc,ocf->ohf', hub_tiles, blocks)
        targets = hub_targets(hub_slots, index).reshape(-1)
        total = total.at[targets].add(part.reshape(-1, WIDTH), mode='drop')
        weight = weight.at[targets].add(lax.optimization_barrier(jnp.sum(hub_tiles, axis=-1)).reshape(-1), mode='drop')
        return (total, weight)
    summed, degree = lax.fori_loop(0, SHARDS, hub_forward, (summed, degree))
    scale = lax.rsqrt(degree + 1.0)
    neigh = (summed * scale[:, None]).astype(jnp.bfloat16)
    pre = jnp.dot(node_feat, self_weight, preferred_element_type=jnp.float32) + jnp.dot(neigh, neigh_weight, preferred_element_type=jnp.float32)
    layer_out = jax.nn.silu(pre).astype(jnp.bfloat16)
    sig = jax.nn.sigmoid(pre)
    slope = sig * (1.0 + pre * (1.0 - sig))
    dpre = (cotangent.astype(jnp.float32) * slope).astype(jnp.bfloat16)
    self_grad = jnp.dot(node_feat.T, dpre, preferred_element_type=jnp.float32)
    neigh_grad = jnp.dot(neigh.T, dpre, preferred_element_type=jnp.float32)
    self_back = jnp.dot(dpre, self_weight.T, preferred_element_type=jnp.float32)
    grad_norm = (jnp.dot(dpre, neigh_weight.T, preferred_element_type=jnp.float32) * scale[:, None]).astype(jnp.bfloat16)
    grads = grad_norm.reshape(N_BLK, N_DOM, BLOCKS_DEV, TILE, WIDTH)
    grads = jnp.concatenate([grads, jnp.zeros((N_BLK, N_DOM, 1, TILE, WIDTH), jnp.bfloat16)], axis=2)
    tiles_all = tile_weights.reshape(N_BLK, N_DOM, N_BLK, SLOTS, TILE, TILE)
    dest_all = tile_dest.reshape(N_BLK, N_DOM, N_BLK, SLOTS)
    source_all = tile_source.reshape(N_BLK, N_DOM, N_BLK, SLOTS)

    def local_backward(index):
        panel_id = index // N_DOM
        dom_id = index % N_DOM
        tiles = tiles_all[:, dom_id, panel_id].astype(jnp.float32)
        dests = dest_all[:, dom_id, panel_id]
        sources = source_all[:, dom_id, panel_id]
        sender_grads = lax.dynamic_index_in_dim(grads, dom_id, 1, False)
        picked = sender_grads[lanes, dests].astype(jnp.float32)
        contrib = jnp.einsum('bkrc,bkrf->bkcf', tiles, picked)
        placing = jax.nn.one_hot(sources, BLOCKS_DEV, dtype=jnp.float32)
        return jnp.einsum('bkn,bkcf->ncf', placing, contrib).reshape(ROWS, WIDTH)
    source_total = lax.map(local_backward, indices).reshape(NODES, WIDTH)
    padded_grad = jnp.concatenate([grad_norm, jnp.zeros((1, WIDTH), jnp.bfloat16)], axis=0)

    def hub_backward(index):
        targets = hub_targets(hub_slots, index)
        picked = padded_grad[targets].astype(jnp.float32)
        contrib = jnp.einsum('ohc,ohf->ocf', hub_weights[index].astype(jnp.float32), picked)
        placing = jax.nn.one_hot(hub_source[index], BLOCKS_DEV, dtype=jnp.float32)
        return jnp.einsum('on,ocf->ncf', placing, contrib).reshape(ROWS, WIDTH)
    hub_total = lax.map(hub_backward, indices).reshape(NODES, WIDTH)
    feat_grad = (self_back + source_total + hub_total).astype(jnp.bfloat16)
    return (layer_out, feat_grad, self_grad, neigh_grad)
```

```python
import functools

import jax
import jax.numpy as jnp
from jax import lax
from jax.experimental import pallas as pl
from jax.experimental.pallas import tpu as pltpu
from jax.sharding import PartitionSpec as P

F32 = jnp.float32
BF16 = jnp.bfloat16
LANES = 128
EXTRA = 8
NT = (((1,), (1,)), ((), ()))
NN = (((1,), (0,)), ((), ()))


def dot(a, b, dims=NN):
    return lax.dot_general(a, b, dims, preferred_element_type=F32)


def call(kernel, out_shape, n_smem, n_vmem, flops, bytes_accessed, scratch=()):
    smem = pl.BlockSpec(memory_space=pltpu.SMEM)
    vmem = pl.BlockSpec(memory_space=pltpu.VMEM)
    return pl.pallas_call(
        kernel,
        out_shape=out_shape,
        in_specs=[smem] * n_smem + [vmem] * n_vmem,
        out_specs=jax.tree.map(lambda _: vmem, out_shape),
        scratch_shapes=list(scratch),
        compiler_params=pltpu.CompilerParams(vmem_limit_bytes=40 << 20),
        cost_estimate=pl.CostEstimate(
            flops=flops, bytes_accessed=bytes_accessed, transcendentals=0
        ),
    )


def shape(dims, dtype):
    return jax.ShapeDtypeStruct(dims, dtype)


def hub_send_kernel(src, w_ref, x_ref, msg_ref, wm_ref):
    owners, hub, tile = w_ref.shape
    nblk = x_ref.shape[0] // tile
    for o in range(owners):
        w = w_ref[o]
        for b in range(nblk):
            wm_ref[o * hub : (o + 1) * hub, b * tile : (b + 1) * tile] = jnp.where(
                src[o] == b, w, jnp.zeros_like(w)
            )
    part = dot(wm_ref[...], x_ref[...]).astype(BF16)
    width = x_ref.shape[1]
    for c in range(width // LANES):
        msg_ref[:, c * hub : (c + 1) * hub, :] = part[:, c * LANES : (c + 1) * LANES].reshape(
            owners, hub, LANES
        )
    flat = w_ref[...].reshape(owners * hub, tile)
    weight = dot(jnp.ones((EXTRA, tile), BF16), flat, NT)
    high = weight.astype(BF16).astype(F32)
    row = lax.broadcasted_iota(jnp.int32, weight.shape, 0)
    pair = jnp.where(row < EXTRA // 2, high, weight - high).astype(BF16)
    per = LANES // hub
    top = (width // LANES) * hub
    for o in range(owners):
        g = o // per
        msg_ref[o, top : top + EXTRA, :] = pair[:, g * LANES : (g + 1) * LANES]


def prepare_kernel(
    dest, source, me, t_ref, wm_ref, row_ref, col_ref, x_ref, sw_ref,
    place_ref, back_ref, onehot_ref, onehot_t_ref, hub_t_ref, xt_ref, xs_ref, deg_ref, pick_ref, mask_ref,
):
    n, tile, _ = t_ref.shape
    rows, width = x_ref.shape
    nblk = rows // tile
    per = back_ref.shape[2] // tile
    for i in range(n):
        t = t_ref[i]
        d = dest[i]
        s = source[i]
        zero = jnp.zeros_like(t)
        tt = t.T
        q, k = i // per, i % per
        for b in range(nblk):
            place_ref[b * tile : (b + 1) * tile, i * tile : (i + 1) * tile] = jnp.where(d == b, t, zero)
            keep = jnp.logical_and(s == b, d < nblk)
            back_ref[q, b * tile : (b + 1) * tile, k * tile : (k + 1) * tile] = jnp.where(keep, tt, zero)
    deg_ref[...] = dot(place_ref[...], jnp.ones((n * tile, LANES), BF16))
    slots = row_ref.shape[1]
    r = lax.broadcasted_iota(jnp.int32, (rows, slots), 0)
    onehot_ref[...] = jnp.where(r == row_ref[...], 1.0, 0.0).astype(BF16)
    c = lax.broadcasted_iota(jnp.int32, (slots, rows), 1)
    onehot_t_ref[...] = jnp.where(c == col_ref[...], 1.0, 0.0).astype(BF16)
    hub_t_ref[...] = wm_ref[...].T
    xt_ref[...] = x_ref[...].T
    xs_ref[...] = dot(x_ref[...], sw_ref[...])
    senders = pick_ref.shape[1]
    hub = slots // senders
    a = lax.broadcasted_iota(jnp.int32, (slots, senders), 0)
    b = lax.broadcasted_iota(jnp.int32, (slots, senders), 1)
    pick_ref[...] = jnp.where(a // hub == b, 1.0, 0.0).astype(BF16)
    a = lax.broadcasted_iota(jnp.int32, (slots, LANES), 0)
    b = lax.broadcasted_iota(jnp.int32, (slots, LANES), 1)
    lane = lax.rem(me[0], LANES // hub) * hub + lax.rem(a, hub)
    mask_ref[...] = jnp.where(b == lane, 1.0, 0.0).astype(BF16)


def tiles_kernel(source, place_ref, halo_ref, out_ref, rhs_ref):
    tile = LANES
    n = place_ref.shape[1] // tile
    panels = halo_ref.shape[0] // (out_ref.shape[0])
    per = n // panels
    nblk = out_ref.shape[0] // tile
    for i in range(n):
        at = pl.multiple_of(((i // per) * nblk + source[i]) * tile, tile)
        rhs_ref[i * tile : (i + 1) * tile, :] = halo_ref[pl.ds(at, tile), :]
    out_ref[...] = dot(place_ref[...], rhs_ref[...])


def middle_kernel(
    got_ref, sum_ref, deg_ref, onehot_ref, onehot_t_ref, pick_ref, mask_ref,
    x_ref, xt_ref, xs_ref, cot_ref, nw_ref,
    out_ref, dpre_ref, gn_ref, wpart_ref, hubg_ref, rhs_ref,
):
    senders, _, _ = got_ref.shape
    rows, width = x_ref.shape
    slots = onehot_ref.shape[1]
    hub = slots // senders
    parts = width // LANES
    for c in range(parts):
        rhs_ref[:, c * LANES : (c + 1) * LANES] = got_ref[:, c * hub : (c + 1) * hub, :].reshape(
            slots, LANES
        )
    top = parts * hub
    for h in range(2):
        line = got_ref[:, top + h * (EXTRA // 2), :]
        spread = dot(pick_ref[...], line).astype(BF16)
        rhs_ref[:, (parts + h) * LANES : (parts + h + 1) * LANES] = spread * mask_ref[...]
    hubs = dot(onehot_ref[...], rhs_ref[...])
    summed = sum_ref[...] + hubs[:, :width]
    hub_deg = jnp.sum(
        hubs[:, width : width + LANES] + hubs[:, width + LANES : width + 2 * LANES],
        axis=1, keepdims=True,
    )
    scale = lax.rsqrt(deg_ref[:, :1] + hub_deg + 1.0)
    neigh = (summed * scale).astype(BF16)
    pre = xs_ref[...] + dot(neigh, nw_ref[...])
    sig = 1.0 / (1.0 + jnp.exp(-pre))
    out_ref[...] = (pre * sig).astype(BF16)
    dpre = (cot_ref[...].astype(F32) * (sig * (1.0 + pre * (1.0 - sig)))).astype(BF16)
    dpre_ref[...] = dpre
    gn = (dot(dpre, nw_ref[...], NT) * scale).astype(BF16)
    gn_ref[...] = gn
    hubg_ref[...] = dot(onehot_t_ref[...], gn).astype(BF16).reshape(hubg_ref.shape)
    wpart_ref[:width, :] = dot(xt_ref[...], dpre)
    wpart_ref[width:, :] = dot(neigh.T, dpre)


def panels_kernel(dest, back_ref, gn_ref, out_ref, rhs_ref):
    panels, rows, depth = back_ref.shape
    tile = LANES
    per = depth // tile
    nblk = rows // tile
    for q in range(panels):
        for k in range(per):
            d = jnp.minimum(dest[q * per + k], nblk - 1)
            at = pl.multiple_of(d * tile, tile)
            rhs_ref[k * tile : (k + 1) * tile, :] = gn_ref[pl.ds(at, tile), :]
        out_ref[q * rows : (q + 1) * rows, :] = dot(back_ref[q], rhs_ref[...])


def final_kernel(panel_ref, back_ref, hub_t_ref, dpre_ref, sw_ref, out_ref):
    slots = hub_t_ref.shape[1]
    width = out_ref.shape[1]
    total = panel_ref[...] + dot(dpre_ref[...], sw_ref[...], NT)
    total = total + dot(hub_t_ref[...], back_ref[...].reshape(slots, width))
    out_ref[...] = total.astype(BF16)


def exchange(x, axis):
    return lax.all_to_all(x, axis, split_axis=0, concat_axis=0, tiled=True)


def sum_everywhere(part, nb, nd):
    depth, width = part.shape
    got = exchange(part.reshape(nb, depth // nb, width), "blk")
    chunk = jnp.sum(got, axis=0)
    got = exchange(chunk.reshape(nd, depth // (nb * nd), width), "dom")
    small = jnp.sum(got, axis=0)
    got = exchange(jnp.broadcast_to(small[None], (nd,) + small.shape), "dom")
    chunk = got.reshape(depth // nb, width)
    got = exchange(jnp.broadcast_to(chunk[None], (nb,) + chunk.shape), "blk")
    return got.reshape(depth, width)


def per_device(
    node_feat, cotangent, self_weight, neigh_weight, tile_weights,
    tile_dest, tile_source, hub_weights, hub_source, hub_slots,
):
    rows, width = node_feat.shape
    _, panels, per, tile, _ = tile_weights.shape
    _, owners, hub, _ = hub_weights.shape
    n = panels * per
    slots = owners * hub
    high = (width // LANES) * hub + EXTRA
    halo = lax.all_gather(node_feat, "blk", axis=0, tiled=True)
    msg, placed_hub = call(
        hub_send_kernel,
        (shape((owners, high, LANES), BF16), shape((slots, rows), BF16)),
        1, 2, 2 * slots * rows * width, 4 << 20,
    )(hub_source[0], hub_weights[0], node_feat)
    got = exchange(msg, "dom")
    dest = tile_dest.reshape(n)
    source = tile_source.reshape(n)
    me = lax.axis_index("dom").astype(jnp.int32).reshape(1)
    slot_row = hub_slots.reshape(1, slots)
    slot_col = hub_slots.reshape(slots, 1)
    place, back, onehot, onehot_t, hub_t, xt, xs, deg, pick, mask = call(
        prepare_kernel,
        (
            shape((rows, n * tile), BF16),
            shape((panels, rows, per * tile), BF16),
            shape((rows, slots), BF16),
            shape((slots, rows), BF16),
            shape((rows, slots), BF16),
            shape((width, rows), BF16),
            shape((rows, width), F32),
            shape((rows, LANES), F32),
            shape((slots, owners), BF16),
            shape((slots, LANES), BF16),
        ),
        3, 6, 2 * rows * n * tile * LANES, 12 << 20,
    )(
        dest, source, me, tile_weights.reshape(n, tile, tile), placed_hub,
        slot_row, slot_col, node_feat, self_weight,
    )
    local = call(
        tiles_kernel, shape((rows, width), F32), 1, 2,
        2 * rows * n * tile * width, 4 << 20, [pltpu.VMEM((n * tile, width), BF16)],
    )(source, place, halo)
    layer_out, dpre, gn, wpart, hub_grad = call(
        middle_kernel,
        (
            shape((rows, width), BF16),
            shape((rows, width), BF16),
            shape((rows, width), BF16),
            shape((2 * width, width), F32),
            shape((owners, hub, width), BF16),
        ),
        0, 12, 6 * slots * rows * width, 8 << 20,
        [pltpu.VMEM((slots, width + 2 * LANES), BF16)],
    )(
        got, local, deg, onehot, onehot_t, pick, mask,
        node_feat, xt, xs, cotangent, neigh_weight,
    )
    back_rows = exchange(hub_grad, "dom")
    terms = call(
        panels_kernel, shape((panels * rows, width), F32), 1, 2,
        2 * rows * n * tile * width, 6 << 20, [pltpu.VMEM((per * tile, width), BF16)],
    )(dest, back, gn)
    panel_total = lax.psum_scatter(terms, "blk", scatter_dimension=0, tiled=True)
    grads = sum_everywhere(wpart, lax.axis_size("blk"), lax.axis_size("dom"))
    feat_grad = call(
        final_kernel, shape((rows, width), BF16), 0, 5,
        2 * slots * rows * width, 4 << 20,
    )(panel_total, back_rows, hub_t, dpre, self_weight)
    return layer_out, feat_grad, grads[:width], grads[width:]


def solution(mesh):
    split = P(("blk", "dom"))
    in_specs = (split, split, P(), P(), split, split, split, split, split, split)
    out_specs = (split, split, P(), P())
    return jax.shard_map(
        per_device, mesh=mesh, in_specs=in_specs, out_specs=out_specs, check_vma=False
    )
```

```python
import jax
import jax.numpy as jnp
from jax import lax
from jax.experimental import pallas as pl
from jax.experimental.pallas import tpu as pltpu
from jax.sharding import Mesh, PartitionSpec as P

F32 = jnp.float32
BF16 = jnp.bfloat16
LANES = 128
EXTRA = 8
SMALL = 1 << 10
TILE_COST = 30_000_000_000
NT = (((1,), (1,)), ((), ()))
NN = (((1,), (0,)), ((), ()))


def dot(a, b, dims=NN):
    return lax.dot_general(a, b, dims, preferred_element_type=F32)


class Arrival:
    def __init__(self, copy, ref):
        self.copy, self.ref = copy, ref

    def __call__(self):
        if self.copy is not None:
            self.copy.wait()
            self.copy = None
        return self.ref


class Departure:
    def __init__(self, copy, ref):
        self.copy, self.ref, self.sent = copy, ref, False

    def send(self):
        self.copy.start()
        self.sent = True


def call(kernel, out_shape, scalars, arrays, scratch=(), flops=SMALL):
    outs = jax.tree.leaves(out_shape)
    n_smem, n_in, n_out = len(scalars), len(arrays), len(outs)

    def body(*refs):
        smem, refs = refs[:n_smem], refs[n_smem:]
        src, refs = refs[:n_in], refs[n_in:]
        dst, refs = refs[:n_out], refs[n_out:]
        held, refs = refs[:n_in], refs[n_in:]
        made, refs = refs[:n_out], refs[n_out:]
        in_sem, out_sem, refs = refs[0], refs[1], refs[2:]
        ins = []
        for i in range(n_in):
            copy = pltpu.make_async_copy(src[i], held[i], in_sem.at[i])
            copy.start()
            ins.append(Arrival(copy, held[i]))
        leaving = [
            Departure(pltpu.make_async_copy(made[i], dst[i], out_sem.at[i]), made[i])
            for i in range(n_out)
        ]
        kernel(*smem, *ins, *leaving, *refs)
        for x in ins:
            x()
        for x in leaving:
            if not x.sent:
                x.send()
        for x in leaving:
            x.copy.wait()

    smem = pl.BlockSpec(memory_space=pltpu.SMEM)
    hbm = pl.BlockSpec(memory_space=pltpu.MemorySpace.HBM)
    buffers = [pltpu.VMEM(x.shape, x.dtype) for x in list(arrays) + outs]
    return pl.pallas_call(
        body,
        out_shape=out_shape,
        in_specs=[smem] * n_smem + [hbm] * n_in,
        out_specs=jax.tree.map(lambda _: hbm, out_shape),
        scratch_shapes=buffers
        + [pltpu.SemaphoreType.DMA((n_in,)), pltpu.SemaphoreType.DMA((n_out,))]
        + list(scratch),
        cost_estimate=pl.CostEstimate(flops=flops, bytes_accessed=SMALL, transcendentals=0),
    )(*scalars, *arrays)


def shape(dims, dtype):
    return jax.ShapeDtypeStruct(dims, dtype)


def hub_send_kernel(src, core, weights, feat, message, placed):
    w_ref, x_ref = weights(), feat()
    msg_ref, wm_ref = message.ref, placed.ref
    owners, hub, tile = w_ref.shape
    width = x_ref.shape[1]
    nblk = x_ref.shape[0] // tile
    half = owners // 2
    for i in range(owners):
        o = (i % half) * 2 + (core[0] if i < half else 1 - core[0])
        w = w_ref[o]
        s = src[o]
        for b in range(nblk):
            wm_ref[i * hub : (i + 1) * hub, b * tile : (b + 1) * tile] = jnp.where(
                s == b, w, jnp.zeros_like(w)
            )
    placed.send()
    part = dot(wm_ref[...], x_ref[...]).astype(BF16)
    for i in range(owners):
        o = (i % half) * 2 + (core[0] if i < half else 1 - core[0])
        for c in range(width // LANES):
            msg_ref[o, c * hub : (c + 1) * hub, :] = part[
                i * hub : (i + 1) * hub, c * LANES : (c + 1) * LANES
            ]
    flat = w_ref[...].reshape(owners * hub, tile)
    weight = dot(jnp.ones((EXTRA, tile), BF16), flat, NT)
    high = weight.astype(BF16).astype(F32)
    row = lax.broadcasted_iota(jnp.int32, weight.shape, 0)
    pair = jnp.where(row < EXTRA // 2, high, weight - high).astype(BF16)
    per = LANES // hub
    top = (width // LANES) * hub
    for o in range(owners):
        g = o // per
        msg_ref[o, top : top + EXTRA, :] = pair[:, g * LANES : (g + 1) * LANES]


def prepare_kernel(
    dest, source, me, tiles, placed_hub, row, col, feat, self_weight,
    place, back, onehot, onehot_t, hub_t, feat_t, feat_self, degree, pick, mask,
):
    t_ref, x_ref = tiles(), feat()
    place_ref, back_ref = place.ref, back.ref
    n, tile, _ = t_ref.shape
    rows, width = x_ref.shape
    nblk = rows // tile
    per = back_ref.shape[2] // tile
    for i in range(n):
        t = t_ref[i]
        d = dest[i]
        s = source[i]
        zero = jnp.zeros_like(t)
        tt = t.T
        q, k = i // per, i % per
        for b in range(nblk):
            place_ref[b * tile : (b + 1) * tile, i * tile : (i + 1) * tile] = jnp.where(d == b, t, zero)
            keep = jnp.logical_and(s == b, d < nblk)
            back_ref[q, b * tile : (b + 1) * tile, k * tile : (k + 1) * tile] = jnp.where(keep, tt, zero)
    place.send()
    back.send()
    degree.ref[...] = dot(place_ref[...], jnp.ones((n * tile, LANES), BF16))
    slots = onehot.ref.shape[1]
    r = lax.broadcasted_iota(jnp.int32, (rows, slots), 0)
    onehot.ref[...] = jnp.where(r == row()[...], 1.0, 0.0).astype(BF16)
    onehot.send()
    c = lax.broadcasted_iota(jnp.int32, (slots, rows), 1)
    onehot_t.ref[...] = jnp.where(c == col()[...], 1.0, 0.0).astype(BF16)
    onehot_t.send()
    hub_t.ref[...] = placed_hub()[...].T
    feat_t.ref[...] = x_ref[...].T
    feat_self.ref[...] = dot(x_ref[...], self_weight()[...])
    senders = pick.ref.shape[1]
    hub = slots // senders
    a = lax.broadcasted_iota(jnp.int32, (slots, senders), 0)
    b = lax.broadcasted_iota(jnp.int32, (slots, senders), 1)
    pick.ref[...] = jnp.where(a // hub == b, 1.0, 0.0).astype(BF16)
    a = lax.broadcasted_iota(jnp.int32, (slots, LANES), 0)
    b = lax.broadcasted_iota(jnp.int32, (slots, LANES), 1)
    lane = lax.rem(me[0], LANES // hub) * hub + lax.rem(a, hub)
    mask.ref[...] = jnp.where(b == lane, 1.0, 0.0).astype(BF16)


def tiles_kernel(source, place, halo, out, rhs_ref):
    halo_ref = halo()
    tile = LANES
    rows = out.ref.shape[0]
    n = place.ref.shape[1] // tile
    per = n // (halo_ref.shape[0] // rows)
    nblk = rows // tile
    for i in range(n):
        at = pl.multiple_of(((i // per) * nblk + source[i]) * tile, tile)
        rhs_ref[i * tile : (i + 1) * tile, :] = halo_ref[pl.ds(at, tile), :]
    out.ref[...] = dot(place()[...], rhs_ref[...])


def middle_kernel(
    core, got, pick, mask, onehot, local, degree, feat_self, neigh_weight, cotangent,
    onehot_t, feat_t,
    layer_out, dpre_out, gn_out, wkeep, wsend, hkeep, hsend, rhs_ref,
):
    got_ref = got()
    senders, _, _ = got_ref.shape
    rows, width = layer_out.ref.shape
    slots = onehot.ref.shape[1]
    hub = slots // senders
    parts = width // LANES
    for c in range(parts):
        rhs_ref[:, c * LANES : (c + 1) * LANES] = got_ref[:, c * hub : (c + 1) * hub, :].reshape(
            slots, LANES
        )
    top = parts * hub
    pick_v, mask_v = pick()[...], mask()[...]
    for h in range(2):
        line = got_ref[:, top + h * (EXTRA // 2), :]
        spread = dot(pick_v, line).astype(BF16)
        rhs_ref[:, (parts + h) * LANES : (parts + h + 1) * LANES] = spread * mask_v
    hubs = dot(onehot()[...], rhs_ref[...])
    summed = local()[...] + hubs[:, :width]
    hub_deg = jnp.sum(
        hubs[:, width : width + LANES] + hubs[:, width + LANES : width + 2 * LANES],
        axis=1, keepdims=True,
    )
    scale = lax.rsqrt(degree()[:, :1] + hub_deg + 1.0)
    neigh = (summed * scale).astype(BF16)
    nw = neigh_weight()[...]
    pre = feat_self()[...] + dot(neigh, nw)
    sig = 1.0 / (1.0 + jnp.exp(-pre))
    dpre = (cotangent()[...].astype(F32) * (sig * (1.0 + pre * (1.0 - sig)))).astype(BF16)
    gn = (dot(dpre, nw, NT) * scale).astype(BF16)
    gn_out.ref[...] = gn
    hot = onehot_t()
    hsend.ref[...] = dot(hot[slots // 2 :, :], gn).astype(BF16).reshape(hsend.ref.shape)
    hsend.send()
    gn_out.send()
    wself = dot(feat_t()[...], dpre)
    wneigh = dot(neigh.T, dpre)
    wsend.ref[...] = jnp.where(core[0] == 0, wneigh, wself)
    wsend.send()
    wkeep.ref[...] = jnp.where(core[0] == 0, wself, wneigh)
    wkeep.send()
    hkeep.ref[...] = dot(hot[: slots // 2, :], gn).astype(BF16).reshape(hkeep.ref.shape)
    hkeep.send()
    layer_out.ref[...] = (pre * sig).astype(BF16)
    dpre_out.ref[...] = dpre


def assemble_kernel(hkeep, hgot, wkeep, wgot, out):
    far, hub, width = hkeep.ref.shape
    out_ref = out.ref
    out_ref[:, :hub, :] = hkeep()[...]
    out_ref[:, hub : 2 * hub, :] = hgot()[...]
    total = wkeep()[...] + wgot()[...]
    high = total.astype(BF16)
    low = (total - high.astype(F32)).astype(BF16)
    rows = total.shape[0] // far
    out_ref[:, 2 * hub : 2 * hub + rows, :] = high.reshape(far, rows, width)
    out_ref[:, 2 * hub + rows :, :] = low.reshape(far, rows, width)


def sum_pairs_kernel(got, out):
    got_ref = got()
    rows = out.ref.shape[1]
    top = got_ref.shape[1] - 2 * rows
    both = got_ref[:, top:, :].astype(F32)
    total = jnp.sum(both[:, :rows, :] + both[:, rows:, :], axis=0)
    out.ref[...] = jnp.broadcast_to(total[None], out.ref.shape)


def sum_kernel(got, out):
    total = jnp.sum(got()[...], axis=0)
    out.ref[...] = jnp.broadcast_to(total[None], out.ref.shape)


def panels_kernel(dest, gn, back, out, rhs_ref):
    gn_ref, back_ref = gn(), back()
    panels, rows, depth = back_ref.shape
    tile = LANES
    per = depth // tile
    nblk = rows // tile
    for q in range(panels):
        for k in range(per):
            d = jnp.minimum(dest[q * per + k], nblk - 1)
            at = pl.multiple_of(d * tile, tile)
            rhs_ref[k * tile : (k + 1) * tile, :] = gn_ref[pl.ds(at, tile), :]
        out.ref[q * rows : (q + 1) * rows, :] = dot(back_ref[q], rhs_ref[...])


def final_kernel(dpre, self_weight, panel, hub_t, back, out):
    back_ref = back()
    slots = hub_t.ref.shape[1]
    width = out.ref.shape[1]
    far = back_ref.shape[0]
    half = slots // 2
    hub = half // far
    hub_ref = hub_t()
    total = panel()[...] + dot(dpre()[...], self_weight()[...], NT)
    for i in range(2):
        rows = back_ref[:, i * hub : (i + 1) * hub, :].reshape(half, width)
        total = total + dot(hub_ref[:, i * half : (i + 1) * half], rows)
    out.ref[...] = total.astype(BF16)


def exchange(x, axis):
    return lax.all_to_all(x, axis, split_axis=0, concat_axis=0, tiled=True)


def swap_cores(x):
    return lax.ppermute(x, "core", [(0, 1), (1, 0)])


def per_device(
    node_feat, cotangent, self_weight, neigh_weight, tile_weights,
    tile_dest, tile_source, hub_weights, hub_source, hub_slots,
):
    rows, width = node_feat.shape
    _, panels, per, tile, _ = tile_weights.shape
    _, owners, hub, _ = hub_weights.shape
    n = panels * per
    slots = owners * hub
    high = (width // LANES) * hub + EXTRA
    nb = lax.axis_size("blk")
    far = lax.axis_size("far")
    core = lax.axis_index("core").astype(jnp.int32)
    halo = lax.all_gather(node_feat, "blk", axis=0, tiled=True)
    msg, placed_hub = call(
        hub_send_kernel,
        (shape((owners, high, LANES), BF16), shape((slots, rows), BF16)),
        (hub_source[0], core.reshape(1)), (hub_weights[0], node_feat),
    )
    got = exchange(msg, ("far", "core"))
    dest = tile_dest.reshape(n)
    source = tile_source.reshape(n)
    me = (lax.axis_index("far") * 2 + core).astype(jnp.int32).reshape(1)
    slot_row = hub_slots.reshape(1, slots)
    pairs = hub_slots.reshape(far, 2, hub)
    pairs = jnp.where(core == 0, pairs, pairs[:, ::-1])
    slot_col = jnp.swapaxes(pairs, 0, 1).reshape(slots, 1)
    place, back, onehot, onehot_t, hub_t, feat_t, feat_self, degree, pick, mask = call(
        prepare_kernel,
        (
            shape((rows, n * tile), BF16),
            shape((panels, rows, per * tile), BF16),
            shape((rows, slots), BF16),
            shape((slots, rows), BF16),
            shape((rows, slots), BF16),
            shape((width, rows), BF16),
            shape((rows, width), F32),
            shape((rows, LANES), F32),
            shape((slots, owners), BF16),
            shape((slots, LANES), BF16),
        ),
        (dest, source, me),
        (
            tile_weights.reshape(n, tile, tile), placed_hub, slot_row, slot_col,
            node_feat, self_weight,
        ),
    )
    local = call(
        tiles_kernel, shape((rows, width), F32), (source,), (place, halo),
        [pltpu.VMEM((n * tile, width), BF16)], TILE_COST,
    )
    square = shape((rows, width), BF16)
    grad_half = shape((width, width), F32)
    hub_half = shape((far, hub, width), BF16)
    layer_out, dpre, gn, wkeep, wsend, hkeep, hsend = call(
        middle_kernel,
        (square, square, square, grad_half, grad_half, hub_half, hub_half),
        (core.reshape(1),),
        (
            got, pick, mask, onehot, local, degree, feat_self, neigh_weight, cotangent,
            onehot_t, feat_t,
        ),
        [pltpu.VMEM((slots, width + 2 * LANES), BF16)],
    )
    chunk = width // far
    packed = call(
        assemble_kernel, shape((far, 2 * (hub + chunk), width), BF16), (),
        (hkeep, swap_cores(hsend), wkeep, swap_cores(wsend)),
    )
    back_rows = exchange(packed, "far")
    terms = call(
        panels_kernel, shape((panels * rows, width), F32), (dest,), (gn, back),
        [pltpu.VMEM((per * tile, width), BF16)],
    )
    panel_total = lax.psum_scatter(terms, "blk", scatter_dimension=0, tiled=True)
    part = call(sum_pairs_kernel, shape((nb, chunk, width), F32), (), (back_rows,))
    total = call(sum_kernel, shape((far, chunk, width), F32), (), (exchange(part, "blk"),))
    mine = exchange(total, "far").reshape(width, width)
    theirs = swap_cores(mine)
    self_grad = jnp.where(core == 0, mine, theirs)
    neigh_grad = jnp.where(core == 0, theirs, mine)
    feat_grad = call(
        final_kernel, square, (), (dpre, self_weight, panel_total, hub_t, back_rows)
    )
    return layer_out, feat_grad, self_grad, neigh_grad


def solution(mesh):
    nb, nd = mesh.devices.shape
    fine = Mesh(mesh.devices.reshape(nb, nd // 2, 2), ("blk", "far", "core"))
    split = P(("blk", "far", "core"))
    in_specs = (split, split, P(), P(), split, split, split, split, split, split)
    out_specs = (split, split, P(), P())
    return jax.shard_map(
        per_device, mesh=fine, in_specs=in_specs, out_specs=out_specs, check_vma=False
    )
```

```python
import jax
import jax.numpy as jnp
from jax import lax
from jax.experimental import pallas as pl
from jax.experimental.pallas import tpu as pltpu
from jax.sharding import Mesh, PartitionSpec as P

F32 = jnp.float32
BF16 = jnp.bfloat16
LANES = 128
EXTRA = 8
SMALL = 1 << 10
TILE_COST = 30_000_000_000
NT = (((1,), (1,)), ((), ()))
NN = (((1,), (0,)), ((), ()))


def dot(a, b, dims=NN):
    return lax.dot_general(a, b, dims, preferred_element_type=F32)


class Arrival:
    def __init__(self, copy, ref):
        self.copy, self.ref = copy, ref

    def __call__(self):
        if self.copy is not None:
            self.copy.wait()
            self.copy = None
        return self.ref


class Departure:
    def __init__(self, copy, ref):
        self.copy, self.ref, self.sent = copy, ref, False

    def send(self):
        self.copy.start()
        self.sent = True


def call(kernel, out_shape, scalars, arrays, scratch=(), flops=SMALL, into=None):
    outs = jax.tree.leaves(out_shape)
    windows = [x[1] if isinstance(x, tuple) else () for x in arrays]
    arrays = [x[0] if isinstance(x, tuple) else x for x in arrays]
    n_smem, n_in, n_out = len(scalars), len(arrays), len(outs)

    def cut(ref, window):
        return ref.at[window] if window else ref

    def body(*refs):
        smem, refs = refs[:n_smem], refs[n_smem:]
        src, refs = refs[:n_in], refs[n_in:]
        if into is not None:
            refs = refs[1:]
        dst, refs = refs[:n_out], refs[n_out:]
        held, refs = refs[:n_in], refs[n_in:]
        made, refs = refs[:n_out], refs[n_out:]
        in_sem, out_sem, refs = refs[0], refs[1], refs[2:]
        ins = []
        for i in range(n_in):
            copy = pltpu.make_async_copy(cut(src[i], windows[i]), held[i], in_sem.at[i])
            copy.start()
            ins.append(Arrival(copy, held[i]))
        leaving = []
        for i in range(n_out):
            there = cut(dst[i], into[1]) if into is not None else dst[i]
            leaving.append(
                Departure(pltpu.make_async_copy(made[i], there, out_sem.at[i]), made[i])
            )
        kernel(*smem, *ins, *leaving, *refs)
        for x in ins:
            x()
        for x in leaving:
            if not x.sent:
                x.send()
        for x in leaving:
            x.copy.wait()

    def size(x, window):
        dims = list(x.shape)
        for i, part in enumerate(window):
            dims[i] = len(range(*part.indices(dims[i])))
        return pltpu.VMEM(tuple(dims), x.dtype)

    smem = pl.BlockSpec(memory_space=pltpu.SMEM)
    hbm = pl.BlockSpec(memory_space=pltpu.MemorySpace.HBM)
    buffers = [size(x, w) for x, w in zip(arrays, windows)]
    buffers += [pltpu.VMEM(x.shape, x.dtype) for x in outs]
    extra = [] if into is None else [into[0]]
    return pl.pallas_call(
        body,
        out_shape=out_shape if into is None else shape(into[0].shape, into[0].dtype),
        in_specs=[smem] * n_smem + [hbm] * (n_in + len(extra)),
        out_specs=jax.tree.map(lambda _: hbm, out_shape),
        scratch_shapes=buffers
        + [pltpu.SemaphoreType.DMA((n_in,)), pltpu.SemaphoreType.DMA((n_out,))]
        + list(scratch),
        input_output_aliases={} if into is None else {n_smem + n_in: 0},
        cost_estimate=pl.CostEstimate(flops=flops, bytes_accessed=SMALL, transcendentals=0),
    )(*scalars, *arrays, *extra)


def shape(dims, dtype):
    return jax.ShapeDtypeStruct(dims, dtype)


def hub_send_kernel(src, core, weights, feat, message, placed):
    w_ref, x_ref = weights(), feat()
    msg_ref, wm_ref = message.ref, placed.ref
    owners, hub, tile = w_ref.shape
    width = x_ref.shape[1]
    nblk = x_ref.shape[0] // tile
    half = owners // 2
    for i in range(owners):
        o = (i % half) * 2 + (core[0] if i < half else 1 - core[0])
        w = w_ref[o]
        s = src[o]
        for b in range(nblk):
            wm_ref[i * hub : (i + 1) * hub, b * tile : (b + 1) * tile] = jnp.where(
                s == b, w, jnp.zeros_like(w)
            )
    placed.send()
    part = dot(wm_ref[...], x_ref[...]).astype(BF16)
    for i in range(owners):
        o = (i % half) * 2 + (core[0] if i < half else 1 - core[0])
        for c in range(width // LANES):
            msg_ref[o, c * hub : (c + 1) * hub, :] = part[
                i * hub : (i + 1) * hub, c * LANES : (c + 1) * LANES
            ]
    flat = w_ref[...].reshape(owners * hub, tile)
    weight = dot(jnp.ones((EXTRA, tile), BF16), flat, NT)
    high = weight.astype(BF16).astype(F32)
    row = lax.broadcasted_iota(jnp.int32, weight.shape, 0)
    pair = jnp.where(row < EXTRA // 2, high, weight - high).astype(BF16)
    per = LANES // hub
    top = (width // LANES) * hub
    for o in range(owners):
        g = o // per
        msg_ref[o, top : top + EXTRA, :] = pair[:, g * LANES : (g + 1) * LANES]


def prepare_kernel(
    dest, source, me, tiles, placed_hub, row, col, feat, self_weight,
    place, back, onehot, onehot_t, hub_t, feat_t, feat_self, degree, pick, mask,
):
    t_ref, x_ref = tiles(), feat()
    place_ref, back_ref = place.ref, back.ref
    n, tile, _ = t_ref.shape
    rows, width = x_ref.shape
    nblk = rows // tile
    per = back_ref.shape[2] // tile
    for i in range(n):
        t = t_ref[i]
        d = dest[i]
        s = source[i]
        zero = jnp.zeros_like(t)
        tt = t.T
        q, k = i // per, i % per
        for b in range(nblk):
            place_ref[b * tile : (b + 1) * tile, i * tile : (i + 1) * tile] = jnp.where(d == b, t, zero)
            keep = jnp.logical_and(s == b, d < nblk)
            back_ref[q, b * tile : (b + 1) * tile, k * tile : (k + 1) * tile] = jnp.where(keep, tt, zero)
    place.send()
    back.send()
    degree.ref[...] = dot(place_ref[...], jnp.ones((n * tile, LANES), BF16))
    slots = onehot.ref.shape[1]
    r = lax.broadcasted_iota(jnp.int32, (rows, slots), 0)
    onehot.ref[...] = jnp.where(r == row()[...], 1.0, 0.0).astype(BF16)
    onehot.send()
    c = lax.broadcasted_iota(jnp.int32, (slots, rows), 1)
    onehot_t.ref[...] = jnp.where(c == col()[...], 1.0, 0.0).astype(BF16)
    onehot_t.send()
    hub_t.ref[...] = placed_hub()[...].T
    feat_t.ref[...] = x_ref[...].T
    feat_self.ref[...] = dot(x_ref[...], self_weight()[...])
    senders = pick.ref.shape[1]
    hub = slots // senders
    a = lax.broadcasted_iota(jnp.int32, (slots, senders), 0)
    b = lax.broadcasted_iota(jnp.int32, (slots, senders), 1)
    pick.ref[...] = jnp.where(a // hub == b, 1.0, 0.0).astype(BF16)
    a = lax.broadcasted_iota(jnp.int32, (slots, LANES), 0)
    b = lax.broadcasted_iota(jnp.int32, (slots, LANES), 1)
    lane = lax.rem(me[0], LANES // hub) * hub + lax.rem(a, hub)
    mask.ref[...] = jnp.where(b == lane, 1.0, 0.0).astype(BF16)


def tiles_kernel(source, here, place, own, beside, *rest):
    pairs, (out, halo_ref, rhs_ref) = rest[:-3], rest[-3:]
    tile = LANES
    rows = out.ref.shape[0]
    n = place.ref.shape[1] // tile
    nx = len(pairs) + 1
    per = n // (2 * nx)
    nblk = rows // tile
    halo_ref[:rows, :] = own()[...]
    halo_ref[rows : 2 * rows, :] = beside()[...]
    for i, pair in enumerate(pairs):
        halo_ref[2 * (i + 1) * rows : 2 * (i + 2) * rows, :] = pair()[...]
    for i in range(n):
        y, x = (i // per) // nx, (i // per) % nx
        back = lax.rem(here[1] - x + nx, nx)
        other = jnp.where(here[0] == y, 0, 1)
        at = pl.multiple_of(((back * 2 + other) * nblk + source[i]) * tile, tile)
        rhs_ref[i * tile : (i + 1) * tile, :] = halo_ref[pl.ds(at, tile), :]
    out.ref[...] = dot(place()[...], rhs_ref[...])


def middle_kernel(
    core, got, pick, mask, onehot, local, degree, feat_self, neigh_weight, cotangent,
    onehot_t, feat_t,
    layer_out, dpre_out, gn_out, wkeep, hkeep, send, rhs_ref,
):
    got_ref = got()
    senders, _, _ = got_ref.shape
    rows, width = layer_out.ref.shape
    slots = onehot.ref.shape[1]
    hub = slots // senders
    parts = width // LANES
    for c in range(parts):
        rhs_ref[:, c * LANES : (c + 1) * LANES] = got_ref[:, c * hub : (c + 1) * hub, :].reshape(
            slots, LANES
        )
    top = parts * hub
    pick_v, mask_v = pick()[...], mask()[...]
    for h in range(2):
        line = got_ref[:, top + h * (EXTRA // 2), :]
        spread = dot(pick_v, line).astype(BF16)
        rhs_ref[:, (parts + h) * LANES : (parts + h + 1) * LANES] = spread * mask_v
    hubs = dot(onehot()[...], rhs_ref[...])
    summed = local()[...] + hubs[:, :width]
    hub_deg = jnp.sum(
        hubs[:, width : width + LANES] + hubs[:, width + LANES : width + 2 * LANES],
        axis=1, keepdims=True,
    )
    scale = lax.rsqrt(degree()[:, :1] + hub_deg + 1.0)
    neigh = (summed * scale).astype(BF16)
    nw = neigh_weight()[...]
    pre = feat_self()[...] + dot(neigh, nw)
    sig = 1.0 / (1.0 + jnp.exp(-pre))
    dpre = (cotangent()[...].astype(F32) * (sig * (1.0 + pre * (1.0 - sig)))).astype(BF16)
    gn = (dot(dpre, nw, NT) * scale).astype(BF16)
    gn_out.ref[...] = gn
    hot = onehot_t()
    wself = dot(feat_t()[...], dpre)
    wneigh = dot(neigh.T, dpre)
    put_pairs(send.ref, hub, jnp.where(core[0] == 0, wneigh, wself))
    send.ref[:, :hub, :] = dot(hot[slots // 2 :, :], gn).astype(BF16).reshape(hkeep.ref.shape)
    send.send()
    gn_out.ref[...] = gn
    gn_out.send()
    wkeep.ref[...] = jnp.where(core[0] == 0, wself, wneigh)
    wkeep.send()
    hkeep.ref[...] = dot(hot[: slots // 2, :], gn).astype(BF16).reshape(hkeep.ref.shape)
    hkeep.send()
    layer_out.ref[...] = (pre * sig).astype(BF16)
    dpre_out.ref[...] = dpre


def put_pairs(ref, top, total):
    far, _, width = ref.shape
    rows = total.shape[0] // far
    high = total.astype(BF16)
    low = (total - high.astype(F32)).astype(BF16)
    ref[:, top : top + rows, :] = high.reshape(far, rows, width)
    ref[:, top + rows : top + 2 * rows, :] = low.reshape(far, rows, width)


def get_pairs(ref, top):
    far, deep, width = ref.shape
    rows = (deep - top) // 2
    both = ref[:, top:, :].astype(F32)
    return both[:, :rows, :] + both[:, rows:, :]


def assemble_kernel(hkeep, wkeep, got, out):
    far, hub, width = hkeep.ref.shape
    out.ref[:, :hub, :] = hkeep()[...]
    got_ref = got()
    out.ref[:, hub : 2 * hub, :] = got_ref[:, :hub, :]
    total = wkeep()[...] + get_pairs(got_ref, hub).reshape(wkeep.ref.shape)
    put_pairs(out.ref, 2 * hub, total)


def sum_rows_kernel(got, out):
    total = jnp.sum(get_pairs(got(), 0), axis=0)
    rows = total.shape[0]
    high = total.astype(BF16)
    low = (total - high.astype(F32)).astype(BF16)
    peers = out.ref.shape[0]
    out.ref[:, :rows, :] = jnp.broadcast_to(high[None], (peers,) + high.shape)
    out.ref[:, rows:, :] = jnp.broadcast_to(low[None], (peers,) + low.shape)


def sum_kernel(got, out):
    total = jnp.sum(get_pairs(got(), 0), axis=0)
    out.ref[...] = jnp.broadcast_to(total[None], out.ref.shape)


def panels_kernel(dest, gn, back, out, rhs_ref):
    gn_ref, back_ref = gn(), back()
    panels, rows, depth = back_ref.shape
    tile = LANES
    per = depth // tile
    nblk = rows // tile
    out.ref[:, rows:, :] = jnp.zeros((panels, out.ref.shape[1] - rows, out.ref.shape[2]), BF16)
    for q in range(panels):
        for k in range(per):
            d = jnp.minimum(dest[q * per + k], nblk - 1)
            at = pl.multiple_of(d * tile, tile)
            rhs_ref[k * tile : (k + 1) * tile, :] = gn_ref[pl.ds(at, tile), :]
        out.ref[q, :rows, :] = dot(back_ref[q], rhs_ref[...]).astype(BF16)


def final_kernel(dpre, self_weight, hub_t, back, terms, out):
    total = dot(dpre()[...], self_weight()[...], NT)
    back_ref, hub_ref = back(), hub_t()
    far, both, width = back_ref.shape
    hub = both // 2
    half = far * hub
    for i in range(2):
        rows = back_ref[:, i * hub : (i + 1) * hub, :].reshape(half, width)
        total = total + dot(hub_ref[:, i * half : (i + 1) * half], rows)
    out.ref[...] = (total + jnp.sum(terms()[...].astype(F32), axis=0)).astype(BF16)


def exchange(x, axis):
    return lax.all_to_all(x, axis, split_axis=0, concat_axis=0, tiled=True)


def swap_cores(x):
    return lax.ppermute(x, "core", [(0, 1), (1, 0)])


def per_device(
    node_feat, cotangent, self_weight, neigh_weight, tile_weights,
    tile_dest, tile_source, hub_weights, hub_source, hub_slots,
):
    rows, width = node_feat.shape
    _, panels, per, tile, _ = tile_weights.shape
    _, owners, hub, _ = hub_weights.shape
    n = panels * per
    slots = owners * hub
    high = (width // LANES) * hub + EXTRA
    far = lax.axis_size("far")
    nx = lax.axis_size("x")
    core = lax.axis_index("core").astype(jnp.int32)
    here = jnp.stack([lax.axis_index("y"), lax.axis_index("x")]).astype(jnp.int32)
    beside = lax.ppermute(node_feat, "y", [(0, 1), (1, 0)])
    msg, placed_hub = call(
        hub_send_kernel,
        (shape((owners, high, LANES), BF16), shape((slots, rows), BF16)),
        (hub_source[0], core.reshape(1)), (hub_weights[0], node_feat),
    )
    got = exchange(msg, ("far", "core"))
    pair, _ = lax.optimization_barrier((jnp.concatenate([node_feat, beside], axis=0), msg))
    pairs = [
        lax.ppermute(pair, "x", [(i, (i + k) % nx) for i in range(nx)]) for k in range(1, nx)
    ]
    dest = tile_dest.reshape(n)
    source = tile_source.reshape(n)
    me = (lax.axis_index("far") * 2 + core).astype(jnp.int32).reshape(1)
    slot_row = hub_slots.reshape(1, slots)
    order = hub_slots.reshape(far, 2, hub)
    order = jnp.where(core == 0, order, order[:, ::-1])
    slot_col = jnp.swapaxes(order, 0, 1).reshape(slots, 1)
    place, back, onehot, onehot_t, hub_t, feat_t, feat_self, degree, pick, mask = call(
        prepare_kernel,
        (
            shape((rows, n * tile), BF16),
            shape((panels, rows, per * tile), BF16),
            shape((rows, slots), BF16),
            shape((slots, rows), BF16),
            shape((rows, slots), BF16),
            shape((width, rows), BF16),
            shape((rows, width), F32),
            shape((rows, LANES), F32),
            shape((slots, owners), BF16),
            shape((slots, LANES), BF16),
        ),
        (dest, source, me),
        (
            tile_weights.reshape(n, tile, tile), placed_hub, slot_row, slot_col,
            node_feat, self_weight,
        ),
    )
    local = call(
        tiles_kernel, shape((rows, width), F32), (source, here),
        (place, node_feat, beside, *pairs),
        [pltpu.VMEM((panels * rows, width), BF16), pltpu.VMEM((n * tile, width), BF16)],
        TILE_COST,
    )
    square = shape((rows, width), BF16)
    chunk = width // far
    layer_out, dpre, gn, wkeep, hkeep, send = call(
        middle_kernel,
        (
            square, square, square, shape((width, width), F32),
            shape((far, hub, width), BF16), shape((far, hub + 2 * chunk, width), BF16),
        ),
        (core.reshape(1),),
        (
            got, pick, mask, onehot, local, degree, feat_self, neigh_weight, cotangent,
            onehot_t, feat_t,
        ),
        [pltpu.VMEM((slots, width + 2 * LANES), BF16)],
    )
    packed = call(
        assemble_kernel, shape((far, 2 * (hub + chunk), width), BF16), (),
        (hkeep, wkeep, swap_cores(send)),
    )
    gathered = exchange(packed, "far")
    gn, _ = lax.optimization_barrier((gn, packed))
    terms = call(
        panels_kernel, shape((panels, rows + 2 * chunk, width), BF16), (dest,), (gn, back),
        [pltpu.VMEM((per * tile, width), BF16)],
    )
    tail = slice(rows, rows + 2 * chunk)
    everything = slice(None)
    terms = call(
        sum_rows_kernel, shape((panels, 2 * chunk, width), BF16), (),
        ((gathered, (everything, slice(2 * hub, 2 * (hub + chunk)))),),
        into=(terms, (everything, tail)),
    )
    terms = exchange(terms, ("y", "x"))
    total = call(
        sum_kernel, shape((far, chunk, width), F32), (), ((terms, (everything, tail)),)
    )
    mine = exchange(total, "far").reshape(width, width)
    theirs = swap_cores(mine)
    self_grad = jnp.where(core == 0, mine, theirs)
    neigh_grad = jnp.where(core == 0, theirs, mine)
    dpre, _ = lax.optimization_barrier((dpre, total))
    feat_grad = call(
        final_kernel, square, (),
        (
            dpre, self_weight, hub_t, (gathered, (everything, slice(0, 2 * hub))),
            (terms, (everything, slice(0, rows))),
        ),
    )
    return layer_out, feat_grad, self_grad, neigh_grad


def solution(mesh):
    nb, nd = mesh.devices.shape
    fine = Mesh(mesh.devices.reshape(2, nb // 2, nd // 2, 2), ("y", "x", "far", "core"))
    split = P(("y", "x", "far", "core"))
    in_specs = (split, split, P(), P(), split, split, split, split, split, split)
    out_specs = (split, split, P(), P())
    return jax.shard_map(
        per_device, mesh=fine, in_specs=in_specs, out_specs=out_specs, check_vma=False
    )
```

```python
import jax
import jax.numpy as jnp
from jax import lax
from jax.experimental import pallas as pl
from jax.experimental.pallas import tpu as pltpu
from jax.sharding import Mesh, PartitionSpec as P

F32 = jnp.float32
BF16 = jnp.bfloat16
LANES = 128
EXTRA = 8
PIECES = 4
SMALL = 1 << 10
TILE_COST = 30_000_000_000
NT = (((1,), (1,)), ((), ()))
NN = (((1,), (0,)), ((), ()))
ALL = slice(None)


def dot(a, b, dims=NN):
    return lax.dot_general(a, b, dims, preferred_element_type=F32)


def shape(dims, dtype):
    return jax.ShapeDtypeStruct(dims, dtype)


class Arrival:
    def __init__(self, copy, ref):
        self.copy, self.ref = copy, ref

    def __call__(self):
        if self.copy is not None:
            self.copy.wait()
            self.copy = None
        return self.ref


class Departure:
    def __init__(self, src, dst, sem):
        self.src, self.dst, self.sem = src, dst, sem
        self.ref, self.copies = src, []

    def send(self, piece=0, pieces=1):
        n = self.src.shape[0] // pieces
        rows = pl.ds(piece * n, n)
        copy = pltpu.make_async_copy(self.src.at[rows], self.dst.at[rows], self.sem.at[piece])
        copy.start()
        self.copies.append(copy)


def call(kernel, outs, scalars, arrays, scratch=(), flops=SMALL, into=None, pieces=1):
    def split(x):
        return x if isinstance(x, tuple) else (x, ())

    def window_shape(x, window):
        dims = list(x.shape)
        for i, part in enumerate(window):
            dims[i] = len(range(*part.indices(dims[i])))
        return pltpu.VMEM(tuple(dims), x.dtype)

    def cut(ref, window):
        return ref.at[window] if window else ref

    arrays, windows = zip(*[split(x) for x in arrays])
    outs = [split(x) for x in outs] if into is None else [into]
    n_smem, n_in, n_out = len(scalars), len(arrays), len(outs)

    def body(*refs):
        smem, refs = refs[:n_smem], refs[n_smem:]
        src, refs = refs[:n_in], refs[n_in:]
        if into is not None:
            refs = refs[1:]
        dst, refs = refs[:n_out], refs[n_out:]
        held, refs = refs[:n_in], refs[n_in:]
        made, refs = refs[:n_out], refs[n_out:]
        in_sem, out_sem, refs = refs[0], refs[1], refs[2:]
        ins = []
        for i in range(n_in):
            copy = pltpu.make_async_copy(cut(src[i], windows[i]), held[i], in_sem.at[i])
            copy.start()
            ins.append(Arrival(copy, held[i]))
        leaving = [
            Departure(made[i], cut(dst[i], outs[i][1]), out_sem.at[i]) for i in range(n_out)
        ]
        kernel(*smem, *ins, *leaving, *refs)
        for x in ins:
            x()
        for x in leaving:
            if not x.copies:
                x.send()
        for x in leaving:
            for copy in x.copies:
                copy.wait()

    smem = pl.BlockSpec(memory_space=pltpu.SMEM)
    hbm = pl.BlockSpec(memory_space=pltpu.MemorySpace.HBM)
    extra = [] if into is None else [into[0]]
    result = pl.pallas_call(
        body,
        out_shape=[shape(x.shape, x.dtype) for x, _ in outs],
        in_specs=[smem] * n_smem + [hbm] * (n_in + len(extra)),
        out_specs=[hbm] * n_out,
        scratch_shapes=[window_shape(x, w) for x, w in zip(arrays, windows)]
        + [window_shape(x, w) for x, w in outs]
        + [pltpu.SemaphoreType.DMA((n_in,)), pltpu.SemaphoreType.DMA((n_out, pieces))]
        + list(scratch),
        input_output_aliases={} if into is None else {n_smem + n_in: 0},
        cost_estimate=pl.CostEstimate(flops=flops, bytes_accessed=SMALL, transcendentals=0),
    )(*scalars, *arrays, *extra)
    return result if n_out > 1 else result[0]


def by_source(w, source, nblk):
    return [jnp.where(source == b, w, jnp.zeros_like(w)) for b in range(nblk)]


def hub_send_kernel(src, weights, feat, message, wm_ref):
    w_ref = weights()
    msg_ref = message.ref
    owners, hub, tile = w_ref.shape
    per = LANES // hub
    flat = w_ref[...].reshape(owners * hub, tile)
    weight = dot(jnp.ones((EXTRA, tile), BF16), flat, NT)
    high = weight.astype(BF16).astype(F32)
    row = lax.broadcasted_iota(jnp.int32, weight.shape, 0)
    pair = jnp.where(row < EXTRA // 2, high, weight - high).astype(BF16)
    x_ref = feat()
    rows, width = x_ref.shape
    nblk = rows // tile
    top = (width // LANES) * hub
    n = owners // PIECES
    for p in range(PIECES):
        for o in range(p * n, (p + 1) * n):
            for b, part in enumerate(by_source(w_ref[o], src[o], nblk)):
                wm_ref[o * hub : (o + 1) * hub, b * tile : (b + 1) * tile] = part
        at = slice(p * n * hub, (p + 1) * n * hub)
        part = dot(wm_ref[at, :], x_ref[...]).astype(BF16)
        for c in range(width // LANES):
            msg_ref[p * n : (p + 1) * n, c * hub : (c + 1) * hub, :] = part[
                :, c * LANES : (c + 1) * LANES
            ].reshape(n, hub, LANES)
        for o in range(p * n, (p + 1) * n):
            g = o // per
            msg_ref[o, top : top + EXTRA, :] = pair[:, g * LANES : (g + 1) * LANES]
        message.send(p, PIECES)


def prepare_kernel(
    dest, source, core, hub_source, tiles, feat, row, col, weights, self_weight,
    place, back, onehot, onehot_t, hub_t, feat_t, feat_self, degree, wm_ref,
):
    t_ref = tiles()
    place_ref, back_ref = place.ref, back.ref
    n, tile, _ = t_ref.shape
    rows = place_ref.shape[0]
    nblk = rows // tile
    per = back_ref.shape[2] // tile
    for i in range(n):
        t = t_ref[i]
        d = dest[i]
        s = source[i]
        zero = jnp.zeros_like(t)
        tt = t.T
        q, k = i // per, i % per
        for b in range(nblk):
            place_ref[b * tile : (b + 1) * tile, i * tile : (i + 1) * tile] = jnp.where(d == b, t, zero)
            keep = jnp.logical_and(s == b, d < nblk)
            back_ref[q, b * tile : (b + 1) * tile, k * tile : (k + 1) * tile] = jnp.where(keep, tt, zero)
    place.send()
    back.send()
    degree.ref[...] = dot(place_ref[...], jnp.ones((n * tile, LANES), BF16))
    degree.send()
    slots = onehot.ref.shape[1]
    r = lax.broadcasted_iota(jnp.int32, (rows, slots), 0)
    onehot.ref[...] = jnp.where(r == row()[...], 1.0, 0.0).astype(BF16)
    onehot.send()
    c = lax.broadcasted_iota(jnp.int32, (slots, rows), 1)
    onehot_t.ref[...] = jnp.where(c == col()[...], 1.0, 0.0).astype(BF16)
    onehot_t.send()
    w_ref = weights()
    owners, hub, _ = w_ref.shape
    half = owners // 2
    for i in range(owners):
        o = (i % half) * 2 + (core[0] if i < half else 1 - core[0])
        for b, part in enumerate(by_source(w_ref[o], hub_source[o], nblk)):
            wm_ref[i * hub : (i + 1) * hub, b * tile : (b + 1) * tile] = part
    hub_t.ref[...] = wm_ref[...].T
    hub_t.send()
    x = feat()[...]
    feat_t.ref[...] = x.T
    feat_self.ref[...] = dot(x, self_weight()[...])


def tiles_kernel(source, here, own, beside, *rest):
    pairs, (place, out, halo_ref, rhs_ref) = rest[:-4], rest[-4:]
    tile = LANES
    rows = out.ref.shape[0]
    n = place.ref.shape[1] // tile
    nx = len(pairs) + 1
    per = n // (2 * nx)
    nblk = rows // tile
    halo_ref[:rows, :] = own()[...]
    halo_ref[rows : 2 * rows, :] = beside()[...]
    for i, pair in enumerate(pairs):
        halo_ref[2 * (i + 1) * rows : 2 * (i + 2) * rows, :] = pair()[...]
    for i in range(n):
        y, x = (i // per) // nx, (i // per) % nx
        back = lax.rem(here[1] - x + nx, nx)
        other = jnp.where(here[0] == y, 0, 1)
        at = pl.multiple_of(((back * 2 + other) * nblk + source[i]) * tile, tile)
        rhs_ref[i * tile : (i + 1) * tile, :] = halo_ref[pl.ds(at, tile), :]
    out.ref[...] = dot(place()[...], rhs_ref[...])


def middle_kernel(
    core, me, got, onehot, local, degree, feat_self, neigh_weight, cotangent, feat_t, onehot_t,
    layer_out, dpre_out, gn_out, wkeep, packed, send, rhs_ref,
):
    got_ref = got()
    senders = got_ref.shape[0]
    rows, width = layer_out.ref.shape
    slots = onehot.ref.shape[1]
    hub = slots // senders
    parts = width // LANES
    for c in range(parts):
        rhs_ref[:, c * LANES : (c + 1) * LANES] = got_ref[:, c * hub : (c + 1) * hub, :].reshape(
            slots, LANES
        )
    top = parts * hub
    slot = lax.broadcasted_iota(jnp.int32, (1, hub, LANES), 1)
    lane = lax.broadcasted_iota(jnp.int32, (1, hub, LANES), 2)
    mine = lane == lax.rem(me[0], LANES // hub) * hub + slot
    for h in range(2):
        line = got_ref[:, top + h * (EXTRA // 2) : top + h * (EXTRA // 2) + 1, :].astype(F32)
        spread = jnp.where(mine, jnp.broadcast_to(line, (senders, hub, LANES)), 0.0)
        rhs_ref[:, (parts + h) * LANES : (parts + h + 1) * LANES] = spread.astype(BF16).reshape(
            slots, LANES
        )
    hubs = dot(onehot()[...], rhs_ref[...])
    summed = local()[...] + hubs[:, :width]
    hub_deg = jnp.sum(
        hubs[:, width : width + LANES] + hubs[:, width + LANES : width + 2 * LANES],
        axis=1, keepdims=True,
    )
    scale = lax.rsqrt(degree()[:, :1] + hub_deg + 1.0)
    neigh = (summed * scale).astype(BF16)
    nw = neigh_weight()[...]
    pre = feat_self()[...] + dot(neigh, nw)
    sig = 1.0 / (1.0 + jnp.exp(-pre))
    dpre = (cotangent()[...].astype(F32) * (sig * (1.0 + pre * (1.0 - sig)))).astype(BF16)
    gn = (dot(dpre, nw, NT) * scale).astype(BF16)
    wself = dot(feat_t()[...], dpre)
    wneigh = dot(neigh.T, dpre)
    put_pairs(send.ref, hub, jnp.where(core[0] == 0, wneigh, wself))
    hot = onehot_t()
    send.ref[:, :hub, :] = dot(hot[slots // 2 :, :], gn).astype(BF16).reshape(packed.ref.shape)
    send.send()
    packed.ref[...] = dot(hot[: slots // 2, :], gn).astype(BF16).reshape(packed.ref.shape)
    packed.send()
    wkeep.ref[...] = jnp.where(core[0] == 0, wself, wneigh)
    wkeep.send()
    gn_out.ref[...] = gn
    gn_out.send()
    layer_out.ref[...] = (pre * sig).astype(BF16)
    dpre_out.ref[...] = dpre


def put_pairs(ref, top, total):
    far, _, width = ref.shape
    rows = total.shape[0] // far
    high = total.astype(BF16)
    low = (total - high.astype(F32)).astype(BF16)
    ref[:, top : top + rows, :] = high.reshape(far, rows, width)
    ref[:, top + rows : top + 2 * rows, :] = low.reshape(far, rows, width)


def get_pairs(ref, top):
    far, deep, width = ref.shape
    rows = (deep - top) // 2
    both = ref[:, top:, :].astype(F32)
    return both[:, :rows, :] + both[:, rows:, :]


def assemble_kernel(got, wkeep, out):
    got_ref = got()
    far, deep, width = got_ref.shape
    hub = deep - 2 * (wkeep.ref.shape[0] // far)
    out.ref[:, :hub, :] = got_ref[:, :hub, :]
    total = wkeep()[...] + get_pairs(got_ref, hub).reshape(wkeep.ref.shape)
    put_pairs(out.ref, hub, total)


def sum_pairs_kernel(got, out):
    total = jnp.sum(get_pairs(got(), 0), axis=0)
    out.ref[...] = jnp.broadcast_to(total[None], out.ref.shape)


def sum_kernel(got, out):
    total = jnp.sum(got()[...], axis=0)
    out.ref[...] = jnp.broadcast_to(total[None], out.ref.shape)


def panels_kernel(dest, here, gn, back, *rest):
    outs, rhs_ref = rest[:-1], rest[-1]
    gn_ref, back_ref = gn(), back()
    panels, rows, depth = back_ref.shape
    tile = LANES
    per = depth // tile
    nblk = rows // tile
    nx = panels // 2
    for step in list(range(1, nx)) + [0]:
        out = outs[step]
        x = lax.rem(here[1] + step, nx)
        for other in range(2):
            q = (here[0] if other == 0 else 1 - here[0]) * nx + x
            for k in range(per):
                d = jnp.minimum(dest[q * per + k], nblk - 1)
                at = pl.multiple_of(d * tile, tile)
                rhs_ref[k * tile : (k + 1) * tile, :] = gn_ref[pl.ds(at, tile), :]
            part = dot(back_ref[q], rhs_ref[...])
            out.ref[other * rows : (other + 1) * rows, :] = part.astype(out.ref.dtype)
        out.send()


def sum_panels_kernel(*rest):
    terms, (here, there) = rest[:-2], rest[-2:]
    rows = here.ref.shape[0]
    total = terms[0]()[...].astype(F32)
    for term in terms[1:]:
        total = total + term()[...].astype(F32)
    there.ref[...] = total[rows:]
    there.send()
    here.ref[...] = total[:rows]


def final_kernel(dpre, self_weight, hub_t, back, here, got, out):
    total = dot(dpre()[...], self_weight()[...], NT)
    back_ref, hub_ref = back(), hub_t()
    far, both, width = back_ref.shape
    hub = both // 2
    half = far * hub
    for i in range(2):
        rows = back_ref[:, i * hub : (i + 1) * hub, :].reshape(half, width)
        total = total + dot(hub_ref[:, i * half : (i + 1) * half], rows)
    out.ref[...] = (total + here()[...] + got()[...]).astype(BF16)


def exchange(x, axis):
    return lax.all_to_all(x, axis, split_axis=0, concat_axis=0, tiled=True)


def swap(x, axis):
    return lax.ppermute(x, axis, [(0, 1), (1, 0)])


def along_x(x, step, nx):
    return lax.ppermute(x, "x", [(i, (i + step) % nx) for i in range(nx)])


def after(x, other):
    return lax.optimization_barrier((x, other))[0]


def per_device(
    node_feat, cotangent, self_weight, neigh_weight, tile_weights,
    tile_dest, tile_source, hub_weights, hub_source, hub_slots,
):
    rows, width = node_feat.shape
    _, panels, per, tile, _ = tile_weights.shape
    _, owners, hub, _ = hub_weights.shape
    n = panels * per
    slots = owners * hub
    high = (width // LANES) * hub + EXTRA
    far = lax.axis_size("far")
    nx = lax.axis_size("x")
    chunk = width // far
    core = lax.axis_index("core").astype(jnp.int32)
    core1 = core.reshape(1)
    me = (lax.axis_index("far") * 2 + core).astype(jnp.int32).reshape(1)
    here = jnp.stack([lax.axis_index("y"), lax.axis_index("x")]).astype(jnp.int32)
    square = shape((rows, width), BF16)
    square32 = shape((rows, width), F32)
    beside = swap(node_feat, "y")
    msg = call(
        hub_send_kernel, [shape((owners, high, LANES), BF16)], (hub_source[0],),
        (hub_weights[0], node_feat), [pltpu.VMEM((slots, rows), BF16)], pieces=PIECES,
    )
    got = exchange(msg, ("far", "core"))
    pair = after(jnp.concatenate([node_feat, beside], axis=0), msg)
    pairs = [along_x(pair, k, nx) for k in range(1, nx)]
    dest = tile_dest.reshape(n)
    source = tile_source.reshape(n)
    slot_row = hub_slots.reshape(1, slots)
    order = hub_slots.reshape(far, 2, hub)
    order = jnp.where(core == 0, order, order[:, ::-1])
    slot_col = jnp.swapaxes(order, 0, 1).reshape(slots, 1)
    place, back, onehot, onehot_t, hub_t, feat_t, feat_self, degree = call(
        prepare_kernel,
        [
            shape((rows, n * tile), BF16),
            shape((panels, rows, per * tile), BF16),
            shape((rows, slots), BF16),
            shape((slots, rows), BF16),
            shape((rows, slots), BF16),
            square,
            square32,
            shape((rows, LANES), F32),
        ],
        (dest, source, core1, hub_source[0]),
        (
            tile_weights.reshape(n, tile, tile), after(node_feat, msg), slot_row, slot_col,
            hub_weights[0], self_weight,
        ),
        [pltpu.VMEM((slots, rows), BF16)],
    )
    local = call(
        tiles_kernel, [square32], (source, here), (node_feat, beside, *pairs, place),
        [pltpu.VMEM((panels * rows, width), BF16), pltpu.VMEM((n * tile, width), BF16)],
        TILE_COST,
    )
    deep = 2 * (hub + chunk)
    layer_out, dpre, gn, wkeep, packed, send = call(
        middle_kernel,
        [
            square, square, square, square32,
            (shape((far, deep, width), BF16), (ALL, slice(0, hub))),
            shape((far, hub + 2 * chunk, width), BF16),
        ],
        (core1, me),
        (
            got, onehot, local, degree, feat_self, neigh_weight, cotangent, feat_t, onehot_t,
        ),
        [pltpu.VMEM((slots, width + 2 * LANES), BF16)],
    )
    packed = call(
        assemble_kernel, [], (), (swap(send, "core"), wkeep),
        into=(packed, (ALL, slice(hub, deep))),
    )
    gathered = exchange(packed, "far")
    terms = call(
        panels_kernel, [shape((2 * rows, width), F32)] + [shape((2 * rows, width), BF16)] * (nx - 1),
        (dest, here), (after(gn, packed), back), [pltpu.VMEM((per * tile, width), BF16)],
    )
    terms = terms if nx > 1 else [terms]
    arrived = [along_x(terms[k], k, nx) for k in range(1, nx)]
    panel_here, panel_there = call(sum_panels_kernel, [square32] * 2, (), (terms[0], *arrived))
    panel_got = swap(panel_there, "y")
    part = call(
        sum_pairs_kernel, [shape((panels, chunk, width), F32)], (),
        ((after(gathered, arrived), (ALL, slice(2 * hub, deep))),),
    )
    total = call(
        sum_kernel, [shape((far, chunk, width), F32)], (), (exchange(part, ("y", "x")),)
    )
    mine = exchange(total, "far").reshape(width, width)
    feat_grad = call(
        final_kernel, [square], (),
        (
            after(dpre, total), self_weight, hub_t, (gathered, (ALL, slice(0, 2 * hub))),
            panel_here, panel_got,
        ),
    )
    theirs = swap(after(mine, feat_grad), "core")
    self_grad = jnp.where(core == 0, mine, theirs)
    neigh_grad = jnp.where(core == 0, theirs, mine)
    return layer_out, feat_grad, self_grad, neigh_grad


def solution(mesh):
    nb, nd = mesh.devices.shape
    fine = Mesh(mesh.devices.reshape(2, nb // 2, nd // 2, 2), ("y", "x", "far", "core"))
    split = P(("y", "x", "far", "core"))
    in_specs = (split, split, P(), P(), split, split, split, split, split, split)
    out_specs = (split, split, P(), P())
    return jax.shard_map(
        per_device, mesh=fine, in_specs=in_specs, out_specs=out_specs, check_vma=False
    )
```

```python
import jax
import jax.numpy as jnp
from jax import lax
from jax.experimental import pallas as pl
from jax.experimental.pallas import tpu as pltpu
from jax.sharding import Mesh, PartitionSpec as P

F32 = jnp.float32
BF16 = jnp.bfloat16
LANES = 128
EXTRA = 8
PIECES = 4
SMALL = 1 << 10
TILE_COST = 30_000_000_000
NT = (((1,), (1,)), ((), ()))
NN = (((1,), (0,)), ((), ()))
ALL = slice(None)


def dot(a, b, dims=NN):
    return lax.dot_general(a, b, dims, preferred_element_type=F32)


def shape(dims, dtype):
    return jax.ShapeDtypeStruct(dims, dtype)


class Arrival:
    def __init__(self, copy, ref):
        self.copy, self.ref = copy, ref

    def __call__(self):
        if self.copy is not None:
            self.copy.wait()
            self.copy = None
        return self.ref


class Departure:
    def __init__(self, src, dst, sem):
        self.src, self.dst, self.sem = src, dst, sem
        self.ref, self.copies = src, []

    def send(self, piece=0, pieces=1):
        n = self.src.shape[0] // pieces
        rows = pl.ds(piece * n, n)
        copy = pltpu.make_async_copy(self.src.at[rows], self.dst.at[rows], self.sem.at[piece])
        copy.start()
        self.copies.append(copy)


def call(kernel, outs, scalars, arrays, scratch=(), flops=SMALL, into=(), pieces=1):
    def split(x):
        return x if isinstance(x, tuple) else (x, ())

    def window_shape(x, window):
        dims = list(x.shape)
        for i, part in enumerate(window):
            dims[i] = len(range(*part.indices(dims[i])))
        return pltpu.VMEM(tuple(dims), x.dtype)

    def cut(ref, window):
        return ref.at[window] if window else ref

    arrays, windows = zip(*[split(x) for x in arrays])
    outs = [split(x) for x in outs] + list(into)
    n_smem, n_in, n_out = len(scalars), len(arrays), len(outs)

    def body(*refs):
        smem, refs = refs[:n_smem], refs[n_smem:]
        src, refs = refs[:n_in], refs[n_in:]
        refs = refs[len(into) :]
        dst, refs = refs[:n_out], refs[n_out:]
        held, refs = refs[:n_in], refs[n_in:]
        made, refs = refs[:n_out], refs[n_out:]
        in_sem, out_sem, refs = refs[0], refs[1], refs[2:]
        ins = []
        for i in range(n_in):
            copy = pltpu.make_async_copy(cut(src[i], windows[i]), held[i], in_sem.at[i])
            copy.start()
            ins.append(Arrival(copy, held[i]))
        leaving = [
            Departure(made[i], cut(dst[i], outs[i][1]), out_sem.at[i]) for i in range(n_out)
        ]
        kernel(*smem, *ins, *leaving, *refs)
        for x in ins:
            x()
        for x in leaving:
            if not x.copies:
                x.send()
        for x in leaving:
            for copy in x.copies:
                copy.wait()

    smem = pl.BlockSpec(memory_space=pltpu.SMEM)
    hbm = pl.BlockSpec(memory_space=pltpu.MemorySpace.HBM)
    extra = [x for x, _ in into]
    first = n_out - len(into)
    result = pl.pallas_call(
        body,
        out_shape=[shape(x.shape, x.dtype) for x, _ in outs],
        in_specs=[smem] * n_smem + [hbm] * (n_in + len(extra)),
        out_specs=[hbm] * n_out,
        scratch_shapes=[window_shape(x, w) for x, w in zip(arrays, windows)]
        + [window_shape(x, w) for x, w in outs]
        + [pltpu.SemaphoreType.DMA((n_in,)), pltpu.SemaphoreType.DMA((n_out, pieces))]
        + list(scratch),
        input_output_aliases={n_smem + n_in + i: first + i for i in range(len(into))},
        cost_estimate=pl.CostEstimate(flops=flops, bytes_accessed=SMALL, transcendentals=0),
    )(*scalars, *arrays, *extra)
    return result if n_out > 1 else result[0]


def by_source(w, source, nblk):
    return [jnp.where(source == b, w, jnp.zeros_like(w)) for b in range(nblk)]


def hub_send_kernel(src, weights, feat, message, wm_ref):
    w_ref = weights()
    msg_ref = message.ref
    owners, hub, tile = w_ref.shape
    per = LANES // hub
    flat = w_ref[...].reshape(owners * hub, tile)
    weight = dot(jnp.ones((EXTRA, tile), BF16), flat, NT)
    high = weight.astype(BF16).astype(F32)
    row = lax.broadcasted_iota(jnp.int32, weight.shape, 0)
    pair = jnp.where(row < EXTRA // 2, high, weight - high).astype(BF16)
    x_ref = feat()
    rows, width = x_ref.shape
    nblk = rows // tile
    top = (width // LANES) * hub
    n = owners // PIECES
    for p in range(PIECES):
        for o in range(p * n, (p + 1) * n):
            for b, part in enumerate(by_source(w_ref[o], src[o], nblk)):
                wm_ref[o * hub : (o + 1) * hub, b * tile : (b + 1) * tile] = part
        at = slice(p * n * hub, (p + 1) * n * hub)
        part = dot(wm_ref[at, :], x_ref[...]).astype(BF16)
        for c in range(width // LANES):
            msg_ref[p * n : (p + 1) * n, c * hub : (c + 1) * hub, :] = part[
                :, c * LANES : (c + 1) * LANES
            ].reshape(n, hub, LANES)
        for o in range(p * n, (p + 1) * n):
            g = o // per
            msg_ref[o, top : top + EXTRA, :] = pair[:, g * LANES : (g + 1) * LANES]
        message.send(p, PIECES)


def prepare_kernel(
    dest, source, core, hub_source, tiles, feat, row, col, weights, self_weight,
    place, back, onehot, onehot_t, hub_t, feat_t, feat_self, degree, wm_ref,
):
    t_ref = tiles()
    place_ref, back_ref = place.ref, back.ref
    n, tile, _ = t_ref.shape
    rows = place_ref.shape[0]
    nblk = rows // tile
    per = back_ref.shape[2] // tile
    for i in range(n):
        t = t_ref[i]
        d = dest[i]
        s = source[i]
        zero = jnp.zeros_like(t)
        tt = t.T
        q, k = i // per, i % per
        for b in range(nblk):
            place_ref[b * tile : (b + 1) * tile, i * tile : (i + 1) * tile] = jnp.where(d == b, t, zero)
            keep = jnp.logical_and(s == b, d < nblk)
            back_ref[q, b * tile : (b + 1) * tile, k * tile : (k + 1) * tile] = jnp.where(keep, tt, zero)
    place.send()
    back.send()
    degree.ref[...] = dot(place_ref[...], jnp.ones((n * tile, LANES), BF16))
    degree.send()
    slots = onehot.ref.shape[1]
    r = lax.broadcasted_iota(jnp.int32, (rows, slots), 0)
    onehot.ref[...] = jnp.where(r == row()[...], 1.0, 0.0).astype(BF16)
    onehot.send()
    c = lax.broadcasted_iota(jnp.int32, (slots, rows), 1)
    onehot_t.ref[...] = jnp.where(c == col()[...], 1.0, 0.0).astype(BF16)
    onehot_t.send()
    w_ref = weights()
    owners, hub, _ = w_ref.shape
    half = owners // 2
    for i in range(owners):
        o = (i % half) * 2 + (core[0] if i < half else 1 - core[0])
        for b, part in enumerate(by_source(w_ref[o], hub_source[o], nblk)):
            wm_ref[i * hub : (i + 1) * hub, b * tile : (b + 1) * tile] = part
    hub_t.ref[...] = wm_ref[...].T
    hub_t.send()
    x = feat()[...]
    feat_t.ref[...] = x.T
    feat_self.ref[...] = dot(x, self_weight()[...])


def tiles_kernel(source, here, own, beside, *rest):
    pairs, (place, out, halo_ref, rhs_ref) = rest[:-4], rest[-4:]
    tile = LANES
    rows = out.ref.shape[0]
    n = place.ref.shape[1] // tile
    nx = len(pairs) + 1
    per = n // (2 * nx)
    nblk = rows // tile
    halo_ref[:rows, :] = own()[...]
    halo_ref[rows : 2 * rows, :] = beside()[...]
    for i, pair in enumerate(pairs):
        halo_ref[2 * (i + 1) * rows : 2 * (i + 2) * rows, :] = pair()[...]
    for i in range(n):
        y, x = (i // per) // nx, (i // per) % nx
        back = lax.rem(here[1] - x + nx, nx)
        other = jnp.where(here[0] == y, 0, 1)
        at = pl.multiple_of(((back * 2 + other) * nblk + source[i]) * tile, tile)
        rhs_ref[i * tile : (i + 1) * tile, :] = halo_ref[pl.ds(at, tile), :]
    out.ref[...] = dot(place()[...], rhs_ref[...])


def middle_kernel(
    core, me, got, onehot, local, degree, feat_self, neigh_weight, cotangent, feat_t, onehot_t,
    layer_out, dpre_out, gn_out, wkeep, wsend, packed, hsend, rhs_ref,
):
    got_ref = got()
    senders = got_ref.shape[0]
    rows, width = layer_out.ref.shape
    slots = onehot.ref.shape[1]
    hub = slots // senders
    parts = width // LANES
    for c in range(parts):
        rhs_ref[:, c * LANES : (c + 1) * LANES] = got_ref[:, c * hub : (c + 1) * hub, :].reshape(
            slots, LANES
        )
    top = parts * hub
    slot = lax.broadcasted_iota(jnp.int32, (1, hub, LANES), 1)
    lane = lax.broadcasted_iota(jnp.int32, (1, hub, LANES), 2)
    mine = lane == lax.rem(me[0], LANES // hub) * hub + slot
    for h in range(2):
        line = got_ref[:, top + h * (EXTRA // 2) : top + h * (EXTRA // 2) + 1, :].astype(F32)
        spread = jnp.where(mine, jnp.broadcast_to(line, (senders, hub, LANES)), 0.0)
        rhs_ref[:, (parts + h) * LANES : (parts + h + 1) * LANES] = spread.astype(BF16).reshape(
            slots, LANES
        )
    hubs = dot(onehot()[...], rhs_ref[...])
    summed = local()[...] + hubs[:, :width]
    hub_deg = jnp.sum(
        hubs[:, width : width + LANES] + hubs[:, width + LANES : width + 2 * LANES],
        axis=1, keepdims=True,
    )
    scale = lax.rsqrt(degree()[:, :1] + hub_deg + 1.0)
    neigh = (summed * scale).astype(BF16)
    nw = neigh_weight()[...]
    pre = feat_self()[...] + dot(neigh, nw)
    sig = 1.0 / (1.0 + jnp.exp(-pre))
    dpre = (cotangent()[...].astype(F32) * (sig * (1.0 + pre * (1.0 - sig)))).astype(BF16)
    gn = (dot(dpre, nw, NT) * scale).astype(BF16)
    wself = dot(feat_t()[...], dpre)
    wneigh = dot(neigh.T, dpre)
    wsend.ref[...] = jnp.where(core[0] == 0, wneigh, wself)
    wsend.send()
    wkeep.ref[...] = jnp.where(core[0] == 0, wself, wneigh)
    wkeep.send()
    gn_out.ref[...] = gn
    gn_out.send()
    hot = onehot_t()
    hsend.ref[...] = dot(hot[slots // 2 :, :], gn).astype(BF16).reshape(hsend.ref.shape)
    hsend.send()
    packed.ref[...] = dot(hot[: slots // 2, :], gn).astype(BF16).reshape(packed.ref.shape)
    packed.send()
    layer_out.ref[...] = (pre * sig).astype(BF16)
    dpre_out.ref[...] = dpre


def add_kernel(got, keep, out):
    total = keep()[...] + got()[...]
    out.ref[...] = total.reshape(out.ref.shape)


def assemble_kernel(got, out):
    out.ref[...] = got()[...]


def panels_kernel(dest, here, gn, back, *rest):
    outs, rhs_ref = rest[:-1], rest[-1]
    gn_ref, back_ref = gn(), back()
    panels, rows, depth = back_ref.shape
    tile = LANES
    per = depth // tile
    nblk = rows // tile
    nx = panels // 2
    for step in list(range(1, nx)) + [0]:
        out = outs[step]
        x = lax.rem(here[1] + step, nx)
        for other in range(2):
            q = (here[0] if other == 0 else 1 - here[0]) * nx + x
            for k in range(per):
                d = jnp.minimum(dest[q * per + k], nblk - 1)
                at = pl.multiple_of(d * tile, tile)
                rhs_ref[k * tile : (k + 1) * tile, :] = gn_ref[pl.ds(at, tile), :]
            part = dot(back_ref[q], rhs_ref[...])
            out.ref[other * rows : (other + 1) * rows, :] = part.astype(out.ref.dtype)
        out.send()


def sum_far_kernel(got, out, *rest):
    total = jnp.sum(got()[...], axis=0)
    rows = total.shape[0]
    high = total.astype(BF16)
    low = (total - high.astype(F32)).astype(BF16)
    for behind in rest:
        behind.ref[:rows, :] = high
        behind.ref[rows:, :] = low
        behind.send()
    out.ref[...] = total


def sum_x_kernel(own, chunk, *rest):
    terms, (here, keep, message) = rest[:-3], rest[-3:]
    rows, small = here.ref.shape[0], keep.ref.shape[0]
    total = own()[...]
    part = chunk()[...]
    for term in terms:
        ref = term()
        total = total + ref[: 2 * rows, :].astype(F32)
        both = ref[2 * rows :, :].astype(F32)
        part = part + (both[:small] + both[small:])
    message.ref[:rows, :] = total[rows:]
    message.ref[rows:, :] = part
    message.send()
    keep.ref[...] = part
    here.ref[...] = total[:rows]


def sum_y_kernel(keep, got, out):
    total = keep()[...] + got()[...]
    out.ref[...] = jnp.broadcast_to(total[None], out.ref.shape)


def final_kernel(dpre, self_weight, hub_t, back, here, got, out):
    total = dot(dpre()[...], self_weight()[...], NT)
    back_ref, hub_ref = back(), hub_t()
    far, both, width = back_ref.shape
    hub = both // 2
    half = far * hub
    for i in range(2):
        rows = back_ref[:, i * hub : (i + 1) * hub, :].reshape(half, width)
        total = total + dot(hub_ref[:, i * half : (i + 1) * half], rows)
    out.ref[...] = (total + here()[...] + got()[...]).astype(BF16)


def square32_pair(rows, width):
    return shape((2 * rows, width), F32)


def as_list(x):
    return list(x) if isinstance(x, (list, tuple)) else [x]


def exchange(x, axis):
    return lax.all_to_all(x, axis, split_axis=0, concat_axis=0, tiled=True)


def swap(x, axis):
    return lax.ppermute(x, axis, [(0, 1), (1, 0)])


def along_x(x, step, nx):
    return lax.ppermute(x, "x", [(i, (i + step) % nx) for i in range(nx)])


def after(x, other):
    return lax.optimization_barrier((x, other))[0]


def per_device(
    node_feat, cotangent, self_weight, neigh_weight, tile_weights,
    tile_dest, tile_source, hub_weights, hub_source, hub_slots,
):
    rows, width = node_feat.shape
    _, panels, per, tile, _ = tile_weights.shape
    _, owners, hub, _ = hub_weights.shape
    n = panels * per
    slots = owners * hub
    high = (width // LANES) * hub + EXTRA
    far = lax.axis_size("far")
    nx = lax.axis_size("x")
    chunk = width // far
    core = lax.axis_index("core").astype(jnp.int32)
    core1 = core.reshape(1)
    me = (lax.axis_index("far") * 2 + core).astype(jnp.int32).reshape(1)
    here = jnp.stack([lax.axis_index("y"), lax.axis_index("x")]).astype(jnp.int32)
    square = shape((rows, width), BF16)
    square32 = shape((rows, width), F32)
    beside = swap(node_feat, "y")
    msg = call(
        hub_send_kernel, [shape((owners, high, LANES), BF16)], (hub_source[0],),
        (hub_weights[0], node_feat), [pltpu.VMEM((slots, rows), BF16)], pieces=PIECES,
    )
    got = exchange(msg, ("far", "core"))
    pair = after(jnp.concatenate([node_feat, beside], axis=0), msg)
    pairs = [along_x(pair, k, nx) for k in range(1, nx)]
    dest = tile_dest.reshape(n)
    source = tile_source.reshape(n)
    slot_row = hub_slots.reshape(1, slots)
    order = hub_slots.reshape(far, 2, hub)
    order = jnp.where(core == 0, order, order[:, ::-1])
    slot_col = jnp.swapaxes(order, 0, 1).reshape(slots, 1)
    place, back, onehot, onehot_t, hub_t, feat_t, feat_self, degree = call(
        prepare_kernel,
        [
            shape((rows, n * tile), BF16),
            shape((panels, rows, per * tile), BF16),
            shape((rows, slots), BF16),
            shape((slots, rows), BF16),
            shape((rows, slots), BF16),
            square,
            square32,
            shape((rows, LANES), F32),
        ],
        (dest, source, core1, hub_source[0]),
        (
            tile_weights.reshape(n, tile, tile), after(node_feat, msg), slot_row, slot_col,
            hub_weights[0], self_weight,
        ),
        [pltpu.VMEM((slots, rows), BF16)],
    )
    local = call(
        tiles_kernel, [square32], (source, here), (node_feat, beside, *pairs, place),
        [pltpu.VMEM((panels * rows, width), BF16), pltpu.VMEM((n * tile, width), BF16)],
        TILE_COST,
    )
    layer_out, dpre, gn, wkeep, wsend, packed, hsend = call(
        middle_kernel,
        [
            square, square, square, square32, square32,
            (shape((far, 2 * hub, width), BF16), (ALL, slice(0, hub))),
            shape((far, hub, width), BF16),
        ],
        (core1, me),
        (
            got, onehot, local, degree, feat_self, neigh_weight, cotangent, feat_t, onehot_t,
        ),
        [pltpu.VMEM((slots, width + 2 * LANES), BF16)],
    )
    both = call(add_kernel, [shape((far, chunk, width), F32)], (), (swap(wsend, "core"), wkeep))
    scattered = exchange(both, "far")
    tall = 2 * rows + 2 * chunk
    terms = call(
        panels_kernel,
        [square32_pair(rows, width)]
        + [(shape((tall, width), BF16), (slice(0, 2 * rows),))] * (nx - 1),
        (dest, here), (after(gn, both), back), [pltpu.VMEM((per * tile, width), BF16)],
    )
    terms = terms if nx > 1 else [terms]
    hsend = after(hsend, both)
    packed = call(
        assemble_kernel, [], (), (swap(hsend, "core"),),
        into=[(packed, (ALL, slice(hub, 2 * hub)))],
    )
    scattered = after(scattered, (terms, packed))
    tail = (slice(2 * rows, tall),)
    part, *behind = as_list(
        call(
            sum_far_kernel, [shape((chunk, width), F32)], (), (scattered,),
            into=[(x, tail) for x in terms[1:]],
        )
    )
    gathered = exchange(after(packed, part), "far")
    arrived = [along_x(behind[k - 1], k, nx) for k in range(1, nx)]
    panel_here, keep, message = call(
        sum_x_kernel, [square32, shape((chunk, width), F32), shape((rows + chunk, width), F32)],
        (), (terms[0], part, *arrived),
    )
    message = swap(message, "y")
    total = call(
        sum_y_kernel, [shape((far, chunk, width), F32)], (),
        (keep, (message, (slice(rows, rows + chunk),))),
    )
    total = after(total, gathered)
    mine = exchange(total, "far").reshape(width, width)
    feat_grad = call(
        final_kernel, [square], (),
        (
            after(dpre, total), self_weight, hub_t, gathered, panel_here,
            (message, (slice(0, rows),)),
        ),
    )
    theirs = swap(after(mine, feat_grad), "core")
    self_grad = jnp.where(core == 0, mine, theirs)
    neigh_grad = jnp.where(core == 0, theirs, mine)
    return layer_out, feat_grad, self_grad, neigh_grad


def solution(mesh):
    nb, nd = mesh.devices.shape
    fine = Mesh(mesh.devices.reshape(2, nb // 2, nd // 2, 2), ("y", "x", "far", "core"))
    split = P(("y", "x", "far", "core"))
    in_specs = (split, split, P(), P(), split, split, split, split, split, split)
    out_specs = (split, split, P(), P())
    return jax.shard_map(
        per_device, mesh=fine, in_specs=in_specs, out_specs=out_specs, check_vma=False
    )
```

```python
import jax
import jax.numpy as jnp
from jax import lax
from jax.experimental import pallas as pl
from jax.experimental.pallas import tpu as pltpu
from jax.sharding import Mesh, PartitionSpec as P

F32 = jnp.float32
BF16 = jnp.bfloat16
LANES = 128
EXTRA = 8
PIECES = 4
SMALL = 1 << 10
TILE_COST = 30_000_000_000
NT = (((1,), (1,)), ((), ()))
NN = (((1,), (0,)), ((), ()))
ALL = slice(None)


def dot(a, b, dims=NN):
    return lax.dot_general(a, b, dims, preferred_element_type=F32)


def shape(dims, dtype):
    return jax.ShapeDtypeStruct(dims, dtype)


class Arrival:
    def __init__(self, copy, ref):
        self.copy, self.ref = copy, ref

    def __call__(self):
        if self.copy is not None:
            self.copy.wait()
            self.copy = None
        return self.ref


class Departure:
    def __init__(self, src, dst, sem):
        self.src, self.dst, self.sem = src, dst, sem
        self.ref, self.copies = src, []

    def send(self, piece=0, pieces=1):
        n = self.src.shape[0] // pieces
        rows = pl.ds(piece * n, n)
        copy = pltpu.make_async_copy(self.src.at[rows], self.dst.at[rows], self.sem.at[piece])
        copy.start()
        self.copies.append(copy)


def call(kernel, outs, scalars, arrays, scratch=(), flops=SMALL, into=(), pieces=1):
    def split(x):
        return x if isinstance(x, tuple) else (x, ())

    def window_shape(x, window):
        dims = list(x.shape)
        for i, part in enumerate(window):
            dims[i] = len(range(*part.indices(dims[i])))
        return pltpu.VMEM(tuple(dims), x.dtype)

    def cut(ref, window):
        return ref.at[window] if window else ref

    arrays, windows = zip(*[split(x) for x in arrays])
    outs = [split(x) for x in outs] + list(into)
    n_smem, n_in, n_out = len(scalars), len(arrays), len(outs)

    def body(*refs):
        smem, refs = refs[:n_smem], refs[n_smem:]
        src, refs = refs[:n_in], refs[n_in:]
        refs = refs[len(into) :]
        dst, refs = refs[:n_out], refs[n_out:]
        held, refs = refs[:n_in], refs[n_in:]
        made, refs = refs[:n_out], refs[n_out:]
        in_sem, out_sem, refs = refs[0], refs[1], refs[2:]
        ins = []
        for i in range(n_in):
            copy = pltpu.make_async_copy(cut(src[i], windows[i]), held[i], in_sem.at[i])
            copy.start()
            ins.append(Arrival(copy, held[i]))
        leaving = [
            Departure(made[i], cut(dst[i], outs[i][1]), out_sem.at[i]) for i in range(n_out)
        ]
        kernel(*smem, *ins, *leaving, *refs)
        for x in ins:
            x()
        for x in leaving:
            if not x.copies:
                x.send()
        for x in leaving:
            for copy in x.copies:
                copy.wait()

    smem = pl.BlockSpec(memory_space=pltpu.SMEM)
    hbm = pl.BlockSpec(memory_space=pltpu.MemorySpace.HBM)
    extra = [x for x, _ in into]
    first = n_out - len(into)
    result = pl.pallas_call(
        body,
        out_shape=[shape(x.shape, x.dtype) for x, _ in outs],
        in_specs=[smem] * n_smem + [hbm] * (n_in + len(extra)),
        out_specs=[hbm] * n_out,
        scratch_shapes=[window_shape(x, w) for x, w in zip(arrays, windows)]
        + [window_shape(x, w) for x, w in outs]
        + [pltpu.SemaphoreType.DMA((n_in,)), pltpu.SemaphoreType.DMA((n_out, pieces))]
        + list(scratch),
        input_output_aliases={n_smem + n_in + i: first + i for i in range(len(into))},
        cost_estimate=pl.CostEstimate(flops=flops, bytes_accessed=SMALL, transcendentals=0),
    )(*scalars, *arrays, *extra)
    return result if n_out > 1 else result[0]


def by_source(w, source, nblk):
    return [jnp.where(source == b, w, jnp.zeros_like(w)) for b in range(nblk)]


def hub_send_kernel(src, weights, feat, message, wm_ref):
    w_ref = weights()
    msg_ref = message.ref
    owners, hub, tile = w_ref.shape
    per = LANES // hub
    flat = w_ref[...].reshape(owners * hub, tile)
    weight = dot(jnp.ones((EXTRA, tile), BF16), flat, NT)
    high = weight.astype(BF16).astype(F32)
    row = lax.broadcasted_iota(jnp.int32, weight.shape, 0)
    pair = jnp.where(row < EXTRA // 2, high, weight - high).astype(BF16)
    x_ref = feat()
    rows, width = x_ref.shape
    nblk = rows // tile
    top = (width // LANES) * hub
    n = owners // PIECES
    for p in range(PIECES):
        for o in range(p * n, (p + 1) * n):
            for b, part in enumerate(by_source(w_ref[o], src[o], nblk)):
                wm_ref[o * hub : (o + 1) * hub, b * tile : (b + 1) * tile] = part
        at = slice(p * n * hub, (p + 1) * n * hub)
        part = dot(wm_ref[at, :], x_ref[...]).astype(BF16)
        for c in range(width // LANES):
            msg_ref[p * n : (p + 1) * n, c * hub : (c + 1) * hub, :] = part[
                :, c * LANES : (c + 1) * LANES
            ].reshape(n, hub, LANES)
        for o in range(p * n, (p + 1) * n):
            g = o // per
            msg_ref[o, top : top + EXTRA, :] = pair[:, g * LANES : (g + 1) * LANES]
        message.send(p, PIECES)


def prepare_kernel(
    dest, source, core, hub_source, tiles, feat, row, col, weights, self_weight,
    place, back, onehot, onehot_t, hub_t, feat_t, feat_self, degree, wm_ref,
):
    t_ref = tiles()
    place_ref, back_ref = place.ref, back.ref
    n, tile, _ = t_ref.shape
    rows = place_ref.shape[0]
    nblk = rows // tile
    per = back_ref.shape[2] // tile
    for i in range(n):
        t = t_ref[i]
        d = dest[i]
        s = source[i]
        zero = jnp.zeros_like(t)
        tt = t.T
        q, k = i // per, i % per
        for b in range(nblk):
            place_ref[b * tile : (b + 1) * tile, i * tile : (i + 1) * tile] = jnp.where(d == b, t, zero)
            keep = jnp.logical_and(s == b, d < nblk)
            back_ref[q, b * tile : (b + 1) * tile, k * tile : (k + 1) * tile] = jnp.where(keep, tt, zero)
    place.send()
    back.send()
    degree.ref[...] = dot(place_ref[...], jnp.ones((n * tile, LANES), BF16))
    degree.send()
    slots = onehot.ref.shape[1]
    r = lax.broadcasted_iota(jnp.int32, (rows, slots), 0)
    onehot.ref[...] = jnp.where(r == row()[...], 1.0, 0.0).astype(BF16)
    onehot.send()
    c = lax.broadcasted_iota(jnp.int32, (slots, rows), 1)
    onehot_t.ref[...] = jnp.where(c == col()[...], 1.0, 0.0).astype(BF16)
    onehot_t.send()
    w_ref = weights()
    owners, hub, _ = w_ref.shape
    half = owners // 2
    for i in range(owners):
        o = (i % half) * 2 + (core[0] if i < half else 1 - core[0])
        for b, part in enumerate(by_source(w_ref[o], hub_source[o], nblk)):
            wm_ref[i * hub : (i + 1) * hub, b * tile : (b + 1) * tile] = part
    hub_t.ref[...] = wm_ref[...].T
    hub_t.send()
    x = feat()[...]
    feat_t.ref[...] = x.T
    feat_self.ref[...] = dot(x, self_weight()[...])


def tiles_kernel(source, here, own, beside, *rest):
    pairs, (place, out, halo_ref, rhs_ref) = rest[:-4], rest[-4:]
    tile = LANES
    rows = out.ref.shape[0]
    n = place.ref.shape[1] // tile
    nx = len(pairs) + 1
    per = n // (2 * nx)
    nblk = rows // tile
    halo_ref[:rows, :] = own()[...]
    halo_ref[rows : 2 * rows, :] = beside()[...]
    for i, pair in enumerate(pairs):
        halo_ref[2 * (i + 1) * rows : 2 * (i + 2) * rows, :] = pair()[...]
    for i in range(n):
        y, x = (i // per) // nx, (i // per) % nx
        back = lax.rem(here[1] - x + nx, nx)
        other = jnp.where(here[0] == y, 0, 1)
        at = pl.multiple_of(((back * 2 + other) * nblk + source[i]) * tile, tile)
        rhs_ref[i * tile : (i + 1) * tile, :] = halo_ref[pl.ds(at, tile), :]
    out.ref[...] = dot(place()[...], rhs_ref[...])


def middle_kernel(
    core, me, got, onehot, local, degree, feat_self, neigh_weight, cotangent, feat_t, onehot_t,
    layer_out, dpre_out, gn_out, wkeep, wsend, packed, hsend, rhs_ref,
):
    got_ref = got()
    senders = got_ref.shape[0]
    rows, width = layer_out.ref.shape
    slots = onehot.ref.shape[1]
    hub = slots // senders
    parts = width // LANES
    for c in range(parts):
        rhs_ref[:, c * LANES : (c + 1) * LANES] = got_ref[:, c * hub : (c + 1) * hub, :].reshape(
            slots, LANES
        )
    top = parts * hub
    slot = lax.broadcasted_iota(jnp.int32, (1, hub, LANES), 1)
    lane = lax.broadcasted_iota(jnp.int32, (1, hub, LANES), 2)
    mine = lane == lax.rem(me[0], LANES // hub) * hub + slot
    for h in range(2):
        line = got_ref[:, top + h * (EXTRA // 2) : top + h * (EXTRA // 2) + 1, :].astype(F32)
        spread = jnp.where(mine, jnp.broadcast_to(line, (senders, hub, LANES)), 0.0)
        rhs_ref[:, (parts + h) * LANES : (parts + h + 1) * LANES] = spread.astype(BF16).reshape(
            slots, LANES
        )
    hubs = dot(onehot()[...], rhs_ref[...])
    summed = local()[...] + hubs[:, :width]
    hub_deg = jnp.sum(
        hubs[:, width : width + LANES] + hubs[:, width + LANES : width + 2 * LANES],
        axis=1, keepdims=True,
    )
    scale = lax.rsqrt(degree()[:, :1] + hub_deg + 1.0)
    neigh = (summed * scale).astype(BF16)
    nw = neigh_weight()[...]
    pre = feat_self()[...] + dot(neigh, nw)
    sig = 1.0 / (1.0 + jnp.exp(-pre))
    dpre = (cotangent()[...].astype(F32) * (sig * (1.0 + pre * (1.0 - sig)))).astype(BF16)
    gn = (dot(dpre, nw, NT) * scale).astype(BF16)
    wself = dot(feat_t()[...], dpre)
    wneigh = dot(neigh.T, dpre)
    wsend.ref[...] = jnp.where(core[0] == 0, wneigh, wself)
    wsend.send()
    wkeep.ref[...] = jnp.where(core[0] == 0, wself, wneigh)
    wkeep.send()
    gn_out.ref[...] = gn
    gn_out.send()
    hot = onehot_t()
    hsend.ref[...] = dot(hot[slots // 2 :, :], gn).astype(BF16).reshape(hsend.ref.shape)
    hsend.send()
    packed.ref[...] = dot(hot[: slots // 2, :], gn).astype(BF16).reshape(packed.ref.shape)
    packed.send()
    layer_out.ref[...] = (pre * sig).astype(BF16)
    dpre_out.ref[...] = dpre


def add_kernel(got, keep, out):
    total = keep()[...] + got()[...]
    wide = total.shape[1] // LANES
    per = out.ref.shape[1] // 8
    for i in range(out.ref.shape[0] * per):
        r, c, k = i // wide, i % wide, i % per
        out.ref[i // per, 8 * k : 8 * (k + 1), :] = total[
            8 * r : 8 * (r + 1), c * LANES : (c + 1) * LANES
        ]


def assemble_kernel(got, out):
    out.ref[...] = got()[...]


def panels_kernel(dest, here, gn, back, *rest):
    outs, rhs_ref = rest[:-1], rest[-1]
    gn_ref, back_ref = gn(), back()
    panels, rows, depth = back_ref.shape
    tile = LANES
    per = depth // tile
    nblk = rows // tile
    nx = panels // 2
    for step in list(range(1, nx)) + [0]:
        out = outs[step]
        x = lax.rem(here[1] + step, nx)
        for other in range(2):
            q = (here[0] if other == 0 else 1 - here[0]) * nx + x
            for k in range(per):
                d = jnp.minimum(dest[q * per + k], nblk - 1)
                at = pl.multiple_of(d * tile, tile)
                rhs_ref[k * tile : (k + 1) * tile, :] = gn_ref[pl.ds(at, tile), :]
            part = dot(back_ref[q], rhs_ref[...])
            out.ref[other * rows : (other + 1) * rows, :] = part.astype(out.ref.dtype)
        out.send()


def sum_far_kernel(got, out, *rest):
    total = jnp.sum(got()[...], axis=0)
    high = total.astype(BF16)
    low = (total - high.astype(F32)).astype(BF16)
    for behind in rest:
        behind.ref[:, :LANES] = high
        behind.ref[:, LANES:] = low
        behind.send()
    out.ref[...] = total


def sum_x_kernel(own, part, *rest):
    messages, (tiles, there, here) = rest[:-3], rest[-3:]
    rows = here.ref.shape[0]
    small = part()[...]
    total = own()[...]
    for message in messages:
        ref = message()
        both = ref[2 * rows :, :].astype(F32)
        small = small + (both[:, :LANES] + both[:, LANES:])
        total = total + ref[: 2 * rows, :].astype(F32)
    tiles.ref[...] = jnp.broadcast_to(small[None], tiles.ref.shape)
    tiles.send()
    there.ref[...] = total[rows:]
    there.send()
    here.ref[...] = total[:rows]


def final_kernel(dpre, self_weight, hub_t, back, here, got, out):
    total = dot(dpre()[...], self_weight()[...], NT)
    back_ref, hub_ref = back(), hub_t()
    far, both, width = back_ref.shape
    hub = both // 2
    half = far * hub
    for i in range(2):
        rows = back_ref[:, i * hub : (i + 1) * hub, :].reshape(half, width)
        total = total + dot(hub_ref[:, i * half : (i + 1) * half], rows)
    out.ref[...] = (total + here()[...] + got()[...]).astype(BF16)


def as_list(x):
    return list(x) if isinstance(x, (list, tuple)) else [x]


def exchange(x, axis):
    return lax.all_to_all(x, axis, split_axis=0, concat_axis=0, tiled=True)


def swap(x, axis):
    return lax.ppermute(x, axis, [(0, 1), (1, 0)])


def along_x(x, step, nx):
    return lax.ppermute(x, "x", [(i, (i + step) % nx) for i in range(nx)])


def after(x, other):
    return lax.optimization_barrier((x, other))[0]


def per_device(
    node_feat, cotangent, self_weight, neigh_weight, tile_weights,
    tile_dest, tile_source, hub_weights, hub_source, hub_slots,
):
    rows, width = node_feat.shape
    _, panels, per, tile, _ = tile_weights.shape
    _, owners, hub, _ = hub_weights.shape
    n = panels * per
    slots = owners * hub
    high = (width // LANES) * hub + EXTRA
    far = lax.axis_size("far")
    nx = lax.axis_size("x")
    core = lax.axis_index("core").astype(jnp.int32)
    core1 = core.reshape(1)
    me = (lax.axis_index("far") * 2 + core).astype(jnp.int32).reshape(1)
    here = jnp.stack([lax.axis_index("y"), lax.axis_index("x")]).astype(jnp.int32)
    square = shape((rows, width), BF16)
    square32 = shape((rows, width), F32)
    beside = swap(node_feat, "y")
    msg = call(
        hub_send_kernel, [shape((owners, high, LANES), BF16)], (hub_source[0],),
        (hub_weights[0], node_feat), [pltpu.VMEM((slots, rows), BF16)], pieces=PIECES,
    )
    got = exchange(msg, ("far", "core"))
    pair = after(jnp.concatenate([node_feat, beside], axis=0), msg)
    pairs = [along_x(pair, k, nx) for k in range(1, nx)]
    dest = tile_dest.reshape(n)
    source = tile_source.reshape(n)
    slot_row = hub_slots.reshape(1, slots)
    order = hub_slots.reshape(far, 2, hub)
    order = jnp.where(core == 0, order, order[:, ::-1])
    slot_col = jnp.swapaxes(order, 0, 1).reshape(slots, 1)
    place, back, onehot, onehot_t, hub_t, feat_t, feat_self, degree = call(
        prepare_kernel,
        [
            shape((rows, n * tile), BF16),
            shape((panels, rows, per * tile), BF16),
            shape((rows, slots), BF16),
            shape((slots, rows), BF16),
            shape((rows, slots), BF16),
            square,
            square32,
            shape((rows, LANES), F32),
        ],
        (dest, source, core1, hub_source[0]),
        (
            tile_weights.reshape(n, tile, tile), after(node_feat, msg), slot_row, slot_col,
            hub_weights[0], self_weight,
        ),
        [pltpu.VMEM((slots, rows), BF16)],
    )
    local = call(
        tiles_kernel, [square32], (source, here), (node_feat, beside, *pairs, place),
        [pltpu.VMEM((panels * rows, width), BF16), pltpu.VMEM((n * tile, width), BF16)],
        TILE_COST,
    )
    layer_out, dpre, gn, wkeep, wsend, packed, hsend = call(
        middle_kernel,
        [
            square, square, square, square32, square32,
            (shape((far, 2 * hub, width), BF16), (ALL, slice(0, hub))),
            shape((far, hub, width), BF16),
        ],
        (core1, me),
        (
            got, onehot, local, degree, feat_self, neigh_weight, cotangent, feat_t, onehot_t,
        ),
        [pltpu.VMEM((slots, width + 2 * LANES), BF16)],
    )
    deep = width * width // (2 * far * LANES)
    tiles = shape((2 * far, deep, LANES), F32)
    both = call(add_kernel, [tiles], (), (swap(wsend, "core"), wkeep))
    scattered = exchange(both, ("y", "far"))
    packed = call(
        assemble_kernel, [], (), (swap(after(hsend, both), "core"),),
        into=[(packed, (ALL, slice(hub, 2 * hub)))],
    )
    tall = 2 * rows + deep
    terms = call(
        panels_kernel,
        [shape((2 * rows, width), F32)]
        + [(shape((tall, width), BF16), (slice(0, 2 * rows),))] * (nx - 1),
        (dest, here), (after(gn, both), back), [pltpu.VMEM((per * tile, width), BF16)],
    )
    terms = [terms] if nx == 1 else terms
    scattered = after(scattered, (terms, packed))
    gathered = exchange(after(packed, scattered), "far")
    tail = (slice(2 * rows, tall),)
    part, *messages = as_list(
        call(
            sum_far_kernel, [shape((deep, LANES), F32)], (), (scattered,),
            into=[(x, tail) for x in terms[1:]],
        )
    )
    arrived = [along_x(messages[k - 1], k, nx) for k in range(1, nx)]
    total, panel_there, panel_here = call(
        sum_x_kernel, [tiles, square32, square32], (), (terms[0], part, *arrived)
    )
    total = after(total, gathered)
    panel_got = swap(after(panel_there, gathered), "y")
    mine = exchange(total, ("y", "far")).reshape(width // 8, width // LANES, 8, LANES)
    mine = jnp.swapaxes(mine, 1, 2).reshape(width, width)
    feat_grad = call(
        final_kernel, [square], (),
        (after(dpre, total), self_weight, hub_t, gathered, panel_here, panel_got),
    )
    theirs = swap(after(mine, feat_grad), "core")
    self_grad = jnp.where(core == 0, mine, theirs)
    neigh_grad = jnp.where(core == 0, theirs, mine)
    return layer_out, feat_grad, self_grad, neigh_grad


def solution(mesh):
    nb, nd = mesh.devices.shape
    fine = Mesh(mesh.devices.reshape(2, nb // 2, nd // 2, 2), ("y", "x", "far", "core"))
    split = P(("y", "x", "far", "core"))
    in_specs = (split, split, P(), P(), split, split, split, split, split, split)
    out_specs = (split, split, P(), P())
    return jax.shard_map(
        per_device, mesh=fine, in_specs=in_specs, out_specs=out_specs, check_vma=False
    )
```

```python
import jax
import jax.numpy as jnp
from jax import lax
from jax.experimental import pallas as pl
from jax.experimental.pallas import tpu as pltpu
from jax.sharding import Mesh, PartitionSpec as P

F32 = jnp.float32
BF16 = jnp.bfloat16
LANES = 128
EXTRA = 8
PIECES = 4
SMALL = 1 << 10
TILE_COST = 30_000_000_000
PANEL_COST = 20_000_000_000
FINAL_COST = 20_000_000_000
NT = (((1,), (1,)), ((), ()))
NN = (((1,), (0,)), ((), ()))
ALL = slice(None)


def dot(a, b, dims=NN):
    return lax.dot_general(a, b, dims, preferred_element_type=F32)


def shape(dims, dtype):
    return jax.ShapeDtypeStruct(dims, dtype)


class Arrival:
    def __init__(self, copy, ref):
        self.copy, self.ref = copy, ref

    def __call__(self):
        if self.copy is not None:
            self.copy.wait()
            self.copy = None
        return self.ref


class Departure:
    def __init__(self, src, dst, sem):
        self.src, self.dst, self.sem = src, dst, sem
        self.ref, self.copies = src, []

    def send(self, piece=0, pieces=1):
        n = self.src.shape[0] // pieces
        rows = pl.ds(piece * n, n)
        copy = pltpu.make_async_copy(self.src.at[rows], self.dst.at[rows], self.sem.at[piece])
        copy.start()
        self.copies.append(copy)


def call(kernel, outs, scalars, arrays, scratch=(), flops=SMALL, into=(), pieces=1):
    def split(x):
        return x if isinstance(x, tuple) else (x, ())

    def window_shape(x, window):
        dims = list(x.shape)
        for i, part in enumerate(window):
            dims[i] = len(range(*part.indices(dims[i])))
        return pltpu.VMEM(tuple(dims), x.dtype)

    def cut(ref, window):
        return ref.at[window] if window else ref

    arrays, windows = zip(*[split(x) for x in arrays])
    outs = [split(x) for x in outs] + list(into)
    n_smem, n_in, n_out = len(scalars), len(arrays), len(outs)

    def body(*refs):
        smem, refs = refs[:n_smem], refs[n_smem:]
        src, refs = refs[:n_in], refs[n_in:]
        refs = refs[len(into) :]
        dst, refs = refs[:n_out], refs[n_out:]
        held, refs = refs[:n_in], refs[n_in:]
        made, refs = refs[:n_out], refs[n_out:]
        in_sem, out_sem, refs = refs[0], refs[1], refs[2:]
        ins = []
        for i in range(n_in):
            copy = pltpu.make_async_copy(cut(src[i], windows[i]), held[i], in_sem.at[i])
            copy.start()
            ins.append(Arrival(copy, held[i]))
        leaving = [
            Departure(made[i], cut(dst[i], outs[i][1]), out_sem.at[i]) for i in range(n_out)
        ]
        kernel(*smem, *ins, *leaving, *refs)
        for x in ins:
            x()
        for x in leaving:
            if not x.copies:
                x.send()
        for x in leaving:
            for copy in x.copies:
                copy.wait()

    smem = pl.BlockSpec(memory_space=pltpu.SMEM)
    hbm = pl.BlockSpec(memory_space=pltpu.MemorySpace.HBM)
    extra = [x for x, _ in into]
    first = n_out - len(into)
    result = pl.pallas_call(
        body,
        out_shape=[shape(x.shape, x.dtype) for x, _ in outs],
        in_specs=[smem] * n_smem + [hbm] * (n_in + len(extra)),
        out_specs=[hbm] * n_out,
        scratch_shapes=[window_shape(x, w) for x, w in zip(arrays, windows)]
        + [window_shape(x, w) for x, w in outs]
        + [pltpu.SemaphoreType.DMA((n_in,)), pltpu.SemaphoreType.DMA((n_out, pieces))]
        + list(scratch),
        input_output_aliases={n_smem + n_in + i: first + i for i in range(len(into))},
        cost_estimate=pl.CostEstimate(flops=flops, bytes_accessed=SMALL, transcendentals=0),
    )(*scalars, *arrays, *extra)
    return result if n_out > 1 else result[0]


def by_source(w, source, nblk):
    return [jnp.where(source == b, w, jnp.zeros_like(w)) for b in range(nblk)]


def hub_send_kernel(src, weights, feat, message, wm_ref):
    w_ref = weights()
    msg_ref = message.ref
    owners, hub, tile = w_ref.shape
    per = LANES // hub
    flat = w_ref[...].reshape(owners * hub, tile)
    weight = dot(jnp.ones((EXTRA, tile), BF16), flat, NT)
    high = weight.astype(BF16).astype(F32)
    row = lax.broadcasted_iota(jnp.int32, weight.shape, 0)
    pair = jnp.where(row < EXTRA // 2, high, weight - high).astype(BF16)
    x_ref = feat()
    rows, width = x_ref.shape
    nblk = rows // tile
    top = (width // LANES) * hub
    n = owners // PIECES
    for p in range(PIECES):
        for o in range(p * n, (p + 1) * n):
            for b, part in enumerate(by_source(w_ref[o], src[o], nblk)):
                wm_ref[o * hub : (o + 1) * hub, b * tile : (b + 1) * tile] = part
        at = slice(p * n * hub, (p + 1) * n * hub)
        part = dot(wm_ref[at, :], x_ref[...]).astype(BF16)
        for c in range(width // LANES):
            msg_ref[p * n : (p + 1) * n, c * hub : (c + 1) * hub, :] = part[
                :, c * LANES : (c + 1) * LANES
            ].reshape(n, hub, LANES)
        for o in range(p * n, (p + 1) * n):
            g = o // per
            msg_ref[o, top : top + EXTRA, :] = pair[:, g * LANES : (g + 1) * LANES]
        message.send(p, PIECES)


def prepare_kernel(
    dest, source, core, hub_source, tiles, feat, row, col, weights, self_weight,
    place, back, onehot, onehot_t, hub_t, feat_t, feat_self, degree, wm_ref,
):
    t_ref = tiles()
    place_ref, back_ref = place.ref, back.ref
    n, tile, _ = t_ref.shape
    rows = place_ref.shape[0]
    nblk = rows // tile
    per = back_ref.shape[2] // tile
    for i in range(n):
        t = t_ref[i]
        d = dest[i]
        s = source[i]
        zero = jnp.zeros_like(t)
        tt = t.T
        q, k = i // per, i % per
        for b in range(nblk):
            place_ref[b * tile : (b + 1) * tile, i * tile : (i + 1) * tile] = jnp.where(d == b, t, zero)
            keep = jnp.logical_and(s == b, d < nblk)
            back_ref[q, b * tile : (b + 1) * tile, k * tile : (k + 1) * tile] = jnp.where(keep, tt, zero)
    place.send()
    back.send()
    degree.ref[...] = dot(place_ref[...], jnp.ones((n * tile, LANES), BF16))
    degree.send()
    slots = onehot.ref.shape[1]
    r = lax.broadcasted_iota(jnp.int32, (rows, slots), 0)
    onehot.ref[...] = jnp.where(r == row()[...], 1.0, 0.0).astype(BF16)
    onehot.send()
    c = lax.broadcasted_iota(jnp.int32, (slots, rows), 1)
    onehot_t.ref[...] = jnp.where(c == col()[...], 1.0, 0.0).astype(BF16)
    onehot_t.send()
    w_ref = weights()
    owners, hub, _ = w_ref.shape
    half = owners // 2
    for i in range(owners):
        o = (i % half) * 2 + (core[0] if i < half else 1 - core[0])
        for b, part in enumerate(by_source(w_ref[o], hub_source[o], nblk)):
            wm_ref[i * hub : (i + 1) * hub, b * tile : (b + 1) * tile] = part
    hub_t.ref[...] = wm_ref[...].T
    hub_t.send()
    x = feat()[...]
    feat_t.ref[...] = x.T
    feat_self.ref[...] = dot(x, self_weight()[...])


def tiles_kernel(source, here, own, beside, *rest):
    pairs, (place, out, halo_ref, rhs_ref) = rest[:-4], rest[-4:]
    tile = LANES
    rows = out.ref.shape[0]
    n = place.ref.shape[1] // tile
    nx = len(pairs) + 1
    per = n // (2 * nx)
    nblk = rows // tile
    halo_ref[:rows, :] = own()[...]
    halo_ref[rows : 2 * rows, :] = beside()[...]
    for i, pair in enumerate(pairs):
        halo_ref[2 * (i + 1) * rows : 2 * (i + 2) * rows, :] = pair()[...]
    for i in range(n):
        y, x = (i // per) // nx, (i // per) % nx
        back = lax.rem(here[1] - x + nx, nx)
        other = jnp.where(here[0] == y, 0, 1)
        at = pl.multiple_of(((back * 2 + other) * nblk + source[i]) * tile, tile)
        rhs_ref[i * tile : (i + 1) * tile, :] = halo_ref[pl.ds(at, tile), :]
    out.ref[...] = dot(place()[...], rhs_ref[...])


def middle_kernel(
    core, me, got, onehot, local, degree, feat_self, neigh_weight, cotangent, feat_t, onehot_t,
    layer_out, dpre_out, gn_out, wkeep, wsend, packed, hsend, rhs_ref,
):
    got_ref = got()
    senders = got_ref.shape[0]
    rows, width = layer_out.ref.shape
    slots = onehot.ref.shape[1]
    hub = slots // senders
    parts = width // LANES
    for c in range(parts):
        rhs_ref[:, c * LANES : (c + 1) * LANES] = got_ref[:, c * hub : (c + 1) * hub, :].reshape(
            slots, LANES
        )
    top = parts * hub
    slot = lax.broadcasted_iota(jnp.int32, (1, hub, LANES), 1)
    lane = lax.broadcasted_iota(jnp.int32, (1, hub, LANES), 2)
    mine = lane == lax.rem(me[0], LANES // hub) * hub + slot
    for h in range(2):
        line = got_ref[:, top + h * (EXTRA // 2) : top + h * (EXTRA // 2) + 1, :].astype(F32)
        spread = jnp.where(mine, jnp.broadcast_to(line, (senders, hub, LANES)), 0.0)
        rhs_ref[:, (parts + h) * LANES : (parts + h + 1) * LANES] = spread.astype(BF16).reshape(
            slots, LANES
        )
    hubs = dot(onehot()[...], rhs_ref[...])
    summed = local()[...] + hubs[:, :width]
    hub_deg = jnp.sum(
        hubs[:, width : width + LANES] + hubs[:, width + LANES : width + 2 * LANES],
        axis=1, keepdims=True,
    )
    scale = lax.rsqrt(degree()[:, :1] + hub_deg + 1.0)
    neigh = (summed * scale).astype(BF16)
    nw = neigh_weight()[...]
    pre = feat_self()[...] + dot(neigh, nw)
    sig = 1.0 / (1.0 + jnp.exp(-pre))
    dpre = (cotangent()[...].astype(F32) * (sig * (1.0 + pre * (1.0 - sig)))).astype(BF16)
    gn = (dot(dpre, nw, NT) * scale).astype(BF16)
    wself = dot(feat_t()[...], dpre)
    wneigh = dot(neigh.T, dpre)
    wsend.ref[...] = jnp.where(core[0] == 0, wneigh, wself)
    wsend.send()
    wkeep.ref[...] = jnp.where(core[0] == 0, wself, wneigh)
    wkeep.send()
    gn_out.ref[...] = gn
    gn_out.send()
    hot = onehot_t()
    hsend.ref[...] = dot(hot[slots // 2 :, :], gn).astype(BF16).reshape(hsend.ref.shape)
    hsend.send()
    packed.ref[...] = dot(hot[: slots // 2, :], gn).astype(BF16).reshape(packed.ref.shape)
    packed.send()
    layer_out.ref[...] = (pre * sig).astype(BF16)
    dpre_out.ref[...] = dpre


def add_kernel(got, keep, out):
    total = keep()[...] + got()[...]
    wide = total.shape[1] // LANES
    per = out.ref.shape[1] // 8
    for i in range(out.ref.shape[0] * per):
        r, c, k = i // wide, i % wide, i % per
        out.ref[i // per, 8 * k : 8 * (k + 1), :] = total[
            8 * r : 8 * (r + 1), c * LANES : (c + 1) * LANES
        ]


def assemble_kernel(got, out):
    out.ref[...] = got()[...]


def panels_kernel(dest, here, gn, back, *rest):
    outs, rhs_ref = rest[:-1], rest[-1]
    gn_ref, back_ref = gn(), back()
    panels, rows, depth = back_ref.shape
    tile = LANES
    per = depth // tile
    nblk = rows // tile
    nx = panels // 2
    for step in list(range(1, nx)) + [0]:
        out = outs[step]
        x = lax.rem(here[1] + step, nx)
        for other in range(2):
            q = (here[0] if other == 0 else 1 - here[0]) * nx + x
            for k in range(per):
                d = jnp.minimum(dest[q * per + k], nblk - 1)
                at = pl.multiple_of(d * tile, tile)
                rhs_ref[k * tile : (k + 1) * tile, :] = gn_ref[pl.ds(at, tile), :]
            part = dot(back_ref[q], rhs_ref[...])
            out.ref[other * rows : (other + 1) * rows, :] = part.astype(out.ref.dtype)
        out.send()


def sum_far_kernel(got, out, *rest):
    total = jnp.sum(got()[...], axis=0)
    high = total.astype(BF16)
    low = (total - high.astype(F32)).astype(BF16)
    for behind in rest:
        behind.ref[:, :LANES] = high
        behind.ref[:, LANES:] = low
        behind.send()
    out.ref[...] = total


def sum_x_kernel(own, part, *rest):
    messages, (tiles, there, here) = rest[:-3], rest[-3:]
    rows = here.ref.shape[0]
    small = part()[...]
    total = own()[...]
    for message in messages:
        ref = message()
        both = ref[2 * rows :, :].astype(F32)
        small = small + (both[:, :LANES] + both[:, LANES:])
        total = total + ref[: 2 * rows, :].astype(F32)
    tiles.ref[...] = jnp.broadcast_to(small[None], tiles.ref.shape)
    tiles.send()
    there.ref[...] = total[rows:]
    there.send()
    here.ref[...] = total[:rows]


def final_kernel(dpre, self_weight, hub_t, back, here, got, out):
    total = dot(dpre()[...], self_weight()[...], NT)
    back_ref, hub_ref = back(), hub_t()
    far, both, width = back_ref.shape
    hub = both // 2
    half = far * hub
    for i in range(2):
        rows = back_ref[:, i * hub : (i + 1) * hub, :].reshape(half, width)
        total = total + dot(hub_ref[:, i * half : (i + 1) * half], rows)
    out.ref[...] = (total + here()[...] + got()[...]).astype(BF16)


def as_list(x):
    return list(x) if isinstance(x, (list, tuple)) else [x]


def exchange(x, axis):
    return lax.all_to_all(x, axis, split_axis=0, concat_axis=0, tiled=True)


def swap(x, axis):
    return lax.ppermute(x, axis, [(0, 1), (1, 0)])


def along_x(x, step, nx):
    return lax.ppermute(x, "x", [(i, (i + step) % nx) for i in range(nx)])


def after(x, other):
    return lax.optimization_barrier((x, other))[0]


def per_device(
    node_feat, cotangent, self_weight, neigh_weight, tile_weights,
    tile_dest, tile_source, hub_weights, hub_source, hub_slots,
):
    rows, width = node_feat.shape
    _, panels, per, tile, _ = tile_weights.shape
    _, owners, hub, _ = hub_weights.shape
    n = panels * per
    slots = owners * hub
    high = (width // LANES) * hub + EXTRA
    far = lax.axis_size("far")
    nx = lax.axis_size("x")
    core = lax.axis_index("core").astype(jnp.int32)
    core1 = core.reshape(1)
    me = (lax.axis_index("far") * 2 + core).astype(jnp.int32).reshape(1)
    here = jnp.stack([lax.axis_index("y"), lax.axis_index("x")]).astype(jnp.int32)
    square = shape((rows, width), BF16)
    square32 = shape((rows, width), F32)
    beside = swap(node_feat, "y")
    msg = call(
        hub_send_kernel, [shape((owners, high, LANES), BF16)], (hub_source[0],),
        (hub_weights[0], node_feat), [pltpu.VMEM((slots, rows), BF16)], pieces=PIECES,
    )
    got = exchange(msg, ("far", "core"))
    pair = after(jnp.concatenate([node_feat, beside], axis=0), msg)
    pairs = [along_x(pair, k, nx) for k in range(1, nx)]
    dest = tile_dest.reshape(n)
    source = tile_source.reshape(n)
    slot_row = hub_slots.reshape(1, slots)
    order = hub_slots.reshape(far, 2, hub)
    order = jnp.where(core == 0, order, order[:, ::-1])
    slot_col = jnp.swapaxes(order, 0, 1).reshape(slots, 1)
    place, back, onehot, onehot_t, hub_t, feat_t, feat_self, degree = call(
        prepare_kernel,
        [
            shape((rows, n * tile), BF16),
            shape((panels, rows, per * tile), BF16),
            shape((rows, slots), BF16),
            shape((slots, rows), BF16),
            shape((rows, slots), BF16),
            square,
            square32,
            shape((rows, LANES), F32),
        ],
        (dest, source, core1, hub_source[0]),
        (
            tile_weights.reshape(n, tile, tile), after(node_feat, msg), slot_row, slot_col,
            hub_weights[0], self_weight,
        ),
        [pltpu.VMEM((slots, rows), BF16)],
    )
    local = call(
        tiles_kernel, [square32], (source, here), (node_feat, beside, *pairs, place),
        [pltpu.VMEM((panels * rows, width), BF16), pltpu.VMEM((n * tile, width), BF16)],
        TILE_COST,
    )
    layer_out, dpre, gn, wkeep, wsend, packed, hsend = call(
        middle_kernel,
        [
            square, square, square, square32, square32,
            (shape((far, 2 * hub, width), BF16), (ALL, slice(0, hub))),
            shape((far, hub, width), BF16),
        ],
        (core1, me),
        (
            got, onehot, local, degree, feat_self, neigh_weight, cotangent, feat_t, onehot_t,
        ),
        [pltpu.VMEM((slots, width + 2 * LANES), BF16)],
    )
    deep = width * width // (2 * far * LANES)
    tiles = shape((2 * far, deep, LANES), F32)
    both = call(add_kernel, [tiles], (), (swap(wsend, "core"), wkeep))
    scattered = exchange(both, ("y", "far"))
    packed = call(
        assemble_kernel, [], (), (swap(after(hsend, both), "core"),),
        into=[(packed, (ALL, slice(hub, 2 * hub)))],
    )
    tall = 2 * rows + deep
    terms = call(
        panels_kernel,
        [shape((2 * rows, width), F32)]
        + [(shape((tall, width), BF16), (slice(0, 2 * rows),))] * (nx - 1),
        (dest, here), (after(gn, both), back), [pltpu.VMEM((per * tile, width), BF16)],
        PANEL_COST,
    )
    terms = [terms] if nx == 1 else terms
    scattered = after(scattered, (terms, packed))
    gathered = exchange(after(packed, scattered), "far")
    tail = (slice(2 * rows, tall),)
    part, *messages = as_list(
        call(
            sum_far_kernel, [shape((deep, LANES), F32)], (), (scattered,),
            into=[(x, tail) for x in terms[1:]],
        )
    )
    arrived = [along_x(messages[k - 1], k, nx) for k in range(1, nx)]
    total, panel_there, panel_here = call(
        sum_x_kernel, [tiles, square32, square32], (), (terms[0], part, *arrived)
    )
    total = after(total, gathered)
    panel_got = swap(after(panel_there, gathered), "y")
    mine = exchange(total, ("y", "far")).reshape(width // 8, width // LANES, 8, LANES)
    mine = jnp.swapaxes(mine, 1, 2).reshape(width, width)
    feat_grad = call(
        final_kernel, [square], (),
        (after(dpre, total), self_weight, hub_t, gathered, panel_here, panel_got),
        flops=FINAL_COST,
    )
    theirs = swap(after(mine, feat_grad), "core")
    self_grad = jnp.where(core == 0, mine, theirs)
    neigh_grad = jnp.where(core == 0, theirs, mine)
    return layer_out, feat_grad, self_grad, neigh_grad


def solution(mesh):
    nb, nd = mesh.devices.shape
    fine = Mesh(mesh.devices.reshape(2, nb // 2, nd // 2, 2), ("y", "x", "far", "core"))
    split = P(("y", "x", "far", "core"))
    in_specs = (split, split, P(), P(), split, split, split, split, split, split)
    out_specs = (split, split, P(), P())
    return jax.shard_map(
        per_device, mesh=fine, in_specs=in_specs, out_specs=out_specs, check_vma=False
    )
```

```python
import jax
import jax.numpy as jnp
from jax import lax
from jax.experimental import pallas as pl
from jax.experimental.pallas import tpu as pltpu
from jax.sharding import Mesh, PartitionSpec as P

F32 = jnp.float32
BF16 = jnp.bfloat16
LANES = 128
EXTRA = 8
PIECES = 2
SMALL = 1 << 10
TILE_COST = 1 << 10
PREPARE_COST = 20_000_000_000
PANEL_COST = 20_000_000_000
FINAL_COST = 20_000_000_000
NT = (((1,), (1,)), ((), ()))
NN = (((1,), (0,)), ((), ()))
ALL = slice(None)


def dot(a, b, dims=NN):
    return lax.dot_general(a, b, dims, preferred_element_type=F32)


def shape(dims, dtype):
    return jax.ShapeDtypeStruct(dims, dtype)


class Arrival:
    def __init__(self, copy, ref):
        self.copy, self.ref = copy, ref

    def __call__(self):
        if self.copy is not None:
            self.copy.wait()
            self.copy = None
        return self.ref


class Departure:
    def __init__(self, src, dst, sem):
        self.src, self.dst, self.sem = src, dst, sem
        self.ref, self.copies = src, []

    def send(self, piece=0, pieces=1):
        n = self.src.shape[0] // pieces
        rows = pl.ds(piece * n, n)
        copy = pltpu.make_async_copy(self.src.at[rows], self.dst.at[rows], self.sem.at[piece])
        copy.start()
        self.copies.append(copy)


def call(kernel, outs, scalars, arrays, scratch=(), flops=SMALL, into=(), pieces=1):
    def split(x):
        return x if isinstance(x, tuple) else (x, ())

    def window_shape(x, window):
        dims = list(x.shape)
        for i, part in enumerate(window):
            dims[i] = len(range(*part.indices(dims[i])))
        return pltpu.VMEM(tuple(dims), x.dtype)

    def cut(ref, window):
        return ref.at[window] if window else ref

    arrays, windows = zip(*[split(x) for x in arrays])
    outs = [split(x) for x in outs] + list(into)
    n_smem, n_in, n_out = len(scalars), len(arrays), len(outs)

    def body(*refs):
        smem, refs = refs[:n_smem], refs[n_smem:]
        src, refs = refs[:n_in], refs[n_in:]
        refs = refs[len(into) :]
        dst, refs = refs[:n_out], refs[n_out:]
        held, refs = refs[:n_in], refs[n_in:]
        made, refs = refs[:n_out], refs[n_out:]
        in_sem, out_sem, refs = refs[0], refs[1], refs[2:]
        ins = []
        for i in range(n_in):
            copy = pltpu.make_async_copy(cut(src[i], windows[i]), held[i], in_sem.at[i])
            copy.start()
            ins.append(Arrival(copy, held[i]))
        leaving = [
            Departure(made[i], cut(dst[i], outs[i][1]), out_sem.at[i]) for i in range(n_out)
        ]
        kernel(*smem, *ins, *leaving, *refs)
        for x in ins:
            x()
        for x in leaving:
            if not x.copies:
                x.send()
        for x in leaving:
            for copy in x.copies:
                copy.wait()

    smem = pl.BlockSpec(memory_space=pltpu.SMEM)
    hbm = pl.BlockSpec(memory_space=pltpu.MemorySpace.HBM)
    extra = [x for x, _ in into]
    first = n_out - len(into)
    result = pl.pallas_call(
        body,
        out_shape=[shape(x.shape, x.dtype) for x, _ in outs],
        in_specs=[smem] * n_smem + [hbm] * (n_in + len(extra)),
        out_specs=[hbm] * n_out,
        scratch_shapes=[window_shape(x, w) for x, w in zip(arrays, windows)]
        + [window_shape(x, w) for x, w in outs]
        + [pltpu.SemaphoreType.DMA((n_in,)), pltpu.SemaphoreType.DMA((n_out, pieces))]
        + list(scratch),
        input_output_aliases={n_smem + n_in + i: first + i for i in range(len(into))},
        cost_estimate=pl.CostEstimate(flops=flops, bytes_accessed=SMALL, transcendentals=0),
    )(*scalars, *arrays, *extra)
    return result if n_out > 1 else result[0]


def by_source(w, source, nblk):
    return [jnp.where(source == b, w, jnp.zeros_like(w)) for b in range(nblk)]


def hub_send_kernel(src, core, weights, feat, packed, send, wm_ref):
    w_ref = weights()
    owners, hub, tile = w_ref.shape
    per = LANES // hub
    flat = w_ref[...].reshape(owners * hub, tile)
    weight = dot(jnp.ones((EXTRA, tile), BF16), flat, NT)
    high = weight.astype(BF16).astype(F32)
    row = lax.broadcasted_iota(jnp.int32, weight.shape, 0)
    pair = jnp.where(row < EXTRA // 2, high, weight - high).astype(BF16)
    x_ref = feat()
    rows, width = x_ref.shape
    nblk = rows // tile
    top = (width // LANES) * hub
    n = owners // 2 // PIECES
    for message, other in ((send, 1 - core[0]), (packed, core[0])):
        msg_ref = message.ref
        for p in range(PIECES):
            for i in range(n):
                o = (p * n + i) * 2 + other
                for b, part in enumerate(by_source(w_ref[o], src[o], nblk)):
                    wm_ref[i * hub : (i + 1) * hub, b * tile : (b + 1) * tile] = part
            part = dot(wm_ref[...], x_ref[...]).astype(BF16)
            for c in range(width // LANES):
                msg_ref[p * n : (p + 1) * n, c * hub : (c + 1) * hub, :] = part[
                    :, c * LANES : (c + 1) * LANES
                ].reshape(n, hub, LANES)
            for i in range(p * n, (p + 1) * n):
                g = 2 * i // per
                msg_ref[i, top : top + EXTRA, :] = pair[:, g * LANES : (g + 1) * LANES]
            message.send(p, PIECES)


def prepare_kernel(
    dest, source, core, hub_source, tiles, feat, row, col, weights, self_weight,
    place, back, onehot, onehot_t, hub_t, feat_t, feat_self, degree, wm_ref,
):
    t_ref = tiles()
    place_ref, back_ref = place.ref, back.ref
    n, tile, _ = t_ref.shape
    rows = place_ref.shape[0]
    nblk = rows // tile
    per = back_ref.shape[2] // tile
    for i in range(n):
        t = t_ref[i]
        d = dest[i]
        s = source[i]
        zero = jnp.zeros_like(t)
        tt = t.T
        q, k = i // per, i % per
        for b in range(nblk):
            place_ref[b * tile : (b + 1) * tile, i * tile : (i + 1) * tile] = jnp.where(d == b, t, zero)
            keep = jnp.logical_and(s == b, d < nblk)
            back_ref[q, b * tile : (b + 1) * tile, k * tile : (k + 1) * tile] = jnp.where(keep, tt, zero)
    place.send()
    back.send()
    degree.ref[...] = dot(place_ref[...], jnp.ones((n * tile, LANES), BF16))
    degree.send()
    slots = onehot.ref.shape[1]
    r = lax.broadcasted_iota(jnp.int32, (rows, slots), 0)
    onehot.ref[...] = jnp.where(r == row()[...], 1.0, 0.0).astype(BF16)
    onehot.send()
    c = lax.broadcasted_iota(jnp.int32, (slots, rows), 1)
    onehot_t.ref[...] = jnp.where(c == col()[...], 1.0, 0.0).astype(BF16)
    onehot_t.send()
    w_ref = weights()
    owners, hub, _ = w_ref.shape
    half = owners // 2
    for i in range(owners):
        o = (i % half) * 2 + (core[0] if i < half else 1 - core[0])
        for b, part in enumerate(by_source(w_ref[o], hub_source[o], nblk)):
            wm_ref[i * hub : (i + 1) * hub, b * tile : (b + 1) * tile] = part
    hub_t.ref[...] = wm_ref[...].T
    hub_t.send()
    x = feat()[...]
    feat_t.ref[...] = x.T
    feat_self.ref[...] = dot(x, self_weight()[...])


def tiles_kernel(source, here, own, beside, *rest):
    pairs, (place, out, halo_ref, rhs_ref) = rest[:-4], rest[-4:]
    tile = LANES
    rows = out.ref.shape[0]
    n = place.ref.shape[1] // tile
    nx = len(pairs) + 1
    per = n // (2 * nx)
    nblk = rows // tile
    halo_ref[:rows, :] = own()[...]
    halo_ref[rows : 2 * rows, :] = beside()[...]
    for i, pair in enumerate(pairs):
        halo_ref[2 * (i + 1) * rows : 2 * (i + 2) * rows, :] = pair()[...]
    for i in range(n):
        y, x = (i // per) // nx, (i // per) % nx
        back = lax.rem(here[1] - x + nx, nx)
        other = jnp.where(here[0] == y, 0, 1)
        at = pl.multiple_of(((back * 2 + other) * nblk + source[i]) * tile, tile)
        rhs_ref[i * tile : (i + 1) * tile, :] = halo_ref[pl.ds(at, tile), :]
    out.ref[...] = dot(place()[...], rhs_ref[...])


def middle_kernel(
    core, me, got, onehot, local, degree, feat_self, neigh_weight, cotangent, feat_t, onehot_t,
    layer_out, dpre_out, gn_out, wkeep, wsend, packed, hsend, rhs_ref,
):
    got_ref = got()
    far, both, _ = got_ref.shape
    rows, width = layer_out.ref.shape
    slots = onehot.ref.shape[1]
    half = slots // 2
    hub = half // far
    parts = width // LANES
    top = parts * hub
    slot = lax.broadcasted_iota(jnp.int32, (1, hub, LANES), 1)
    lane = lax.broadcasted_iota(jnp.int32, (1, hub, LANES), 2)
    mine = lane == lax.rem(me[0], LANES // hub) * hub + slot
    for r in range(2):
        at, base = slice(r * half, (r + 1) * half), r * (both // 2)
        for c in range(parts):
            rhs_ref[at, c * LANES : (c + 1) * LANES] = got_ref[
                :, base + c * hub : base + (c + 1) * hub, :
            ].reshape(half, LANES)
        for h in range(2):
            first = base + top + h * (EXTRA // 2)
            line = got_ref[:, first : first + 1, :].astype(F32)
            spread = jnp.where(mine, jnp.broadcast_to(line, (far, hub, LANES)), 0.0)
            rhs_ref[at, (parts + h) * LANES : (parts + h + 1) * LANES] = spread.astype(
                BF16
            ).reshape(half, LANES)
    hubs = dot(onehot()[...], rhs_ref[...])
    summed = local()[...] + hubs[:, :width]
    hub_deg = jnp.sum(
        hubs[:, width : width + LANES] + hubs[:, width + LANES : width + 2 * LANES],
        axis=1, keepdims=True,
    )
    scale = lax.rsqrt(degree()[:, :1] + hub_deg + 1.0)
    neigh = (summed * scale).astype(BF16)
    nw = neigh_weight()[...]
    pre = feat_self()[...] + dot(neigh, nw)
    sig = 1.0 / (1.0 + jnp.exp(-pre))
    dpre = (cotangent()[...].astype(F32) * (sig * (1.0 + pre * (1.0 - sig)))).astype(BF16)
    gn = (dot(dpre, nw, NT) * scale).astype(BF16)
    wself = dot(feat_t()[...], dpre)
    wneigh = dot(neigh.T, dpre)
    wsend.ref[...] = jnp.where(core[0] == 0, wneigh, wself)
    wsend.send()
    wkeep.ref[...] = jnp.where(core[0] == 0, wself, wneigh)
    wkeep.send()
    gn_out.ref[...] = gn
    gn_out.send()
    hot = onehot_t()
    hsend.ref[...] = dot(hot[slots // 2 :, :], gn).astype(BF16).reshape(hsend.ref.shape)
    hsend.send()
    packed.ref[...] = dot(hot[: slots // 2, :], gn).astype(BF16).reshape(packed.ref.shape)
    packed.send()
    layer_out.ref[...] = (pre * sig).astype(BF16)
    dpre_out.ref[...] = dpre


def add_kernel(got, keep, out):
    total = keep()[...] + got()[...]
    wide = total.shape[1] // LANES
    per = out.ref.shape[1] // 8
    for i in range(out.ref.shape[0] * per):
        r, c, k = i // wide, i % wide, i % per
        out.ref[i // per, 8 * k : 8 * (k + 1), :] = total[
            8 * r : 8 * (r + 1), c * LANES : (c + 1) * LANES
        ]


def assemble_kernel(got, out):
    out.ref[...] = got()[...]


def panels_kernel(dest, here, gn, back, *rest):
    outs, rhs_ref = rest[:-1], rest[-1]
    gn_ref, back_ref = gn(), back()
    panels, rows, depth = back_ref.shape
    tile = LANES
    per = depth // tile
    nblk = rows // tile
    nx = panels // 2
    for step in list(range(1, nx)) + [0]:
        out = outs[step]
        x = lax.rem(here[1] + step, nx)
        for other in range(2):
            q = (here[0] if other == 0 else 1 - here[0]) * nx + x
            for k in range(per):
                d = jnp.minimum(dest[q * per + k], nblk - 1)
                at = pl.multiple_of(d * tile, tile)
                rhs_ref[k * tile : (k + 1) * tile, :] = gn_ref[pl.ds(at, tile), :]
            part = dot(back_ref[q], rhs_ref[...])
            out.ref[other * rows : (other + 1) * rows, :] = part.astype(out.ref.dtype)
        out.send()


def sum_far_kernel(got, out, *rest):
    total = jnp.sum(got()[...], axis=0)
    high = total.astype(BF16)
    low = (total - high.astype(F32)).astype(BF16)
    for behind in rest:
        behind.ref[:, :LANES] = high
        behind.ref[:, LANES:] = low
        behind.send()
    out.ref[...] = total


def sum_x_kernel(own, part, *rest):
    messages, (tiles, there, here) = rest[:-3], rest[-3:]
    rows = here.ref.shape[0]
    small = part()[...]
    total = own()[...]
    for message in messages:
        ref = message()
        both = ref[2 * rows :, :].astype(F32)
        small = small + (both[:, :LANES] + both[:, LANES:])
        total = total + ref[: 2 * rows, :].astype(F32)
    tiles.ref[...] = jnp.broadcast_to(small[None], tiles.ref.shape)
    tiles.send()
    there.ref[...] = total[rows:]
    there.send()
    here.ref[...] = total[:rows]


def final_kernel(dpre, self_weight, hub_t, back, here, got, out):
    total = dot(dpre()[...], self_weight()[...], NT)
    back_ref, hub_ref = back(), hub_t()
    far, both, width = back_ref.shape
    hub = both // 2
    half = far * hub
    for i in range(2):
        rows = back_ref[:, i * hub : (i + 1) * hub, :].reshape(half, width)
        total = total + dot(hub_ref[:, i * half : (i + 1) * half], rows)
    out.ref[...] = (total + here()[...] + got()[...]).astype(BF16)


def as_list(x):
    return list(x) if isinstance(x, (list, tuple)) else [x]


def exchange(x, axis):
    return lax.all_to_all(x, axis, split_axis=0, concat_axis=0, tiled=True)


def swap(x, axis):
    return lax.ppermute(x, axis, [(0, 1), (1, 0)])


def along_x(x, step, nx):
    return lax.ppermute(x, "x", [(i, (i + step) % nx) for i in range(nx)])


def after(x, other):
    return lax.optimization_barrier((x, other))[0]


def per_device(
    node_feat, cotangent, self_weight, neigh_weight, tile_weights,
    tile_dest, tile_source, hub_weights, hub_source, hub_slots,
):
    rows, width = node_feat.shape
    _, panels, per, tile, _ = tile_weights.shape
    _, owners, hub, _ = hub_weights.shape
    n = panels * per
    slots = owners * hub
    high = (width // LANES) * hub + EXTRA
    far = lax.axis_size("far")
    nx = lax.axis_size("x")
    core = lax.axis_index("core").astype(jnp.int32)
    core1 = core.reshape(1)
    me = (lax.axis_index("far") * 2 + core).astype(jnp.int32).reshape(1)
    here = jnp.stack([lax.axis_index("y"), lax.axis_index("x")]).astype(jnp.int32)
    square = shape((rows, width), BF16)
    square32 = shape((rows, width), F32)
    beside = swap(node_feat, "y")
    msg, send = call(
        hub_send_kernel,
        [
            (shape((far, 2 * high, LANES), BF16), (ALL, slice(0, high))),
            shape((far, high, LANES), BF16),
        ],
        (hub_source[0], core1), (hub_weights[0], node_feat),
        [pltpu.VMEM((slots // 2 // PIECES, rows), BF16)], pieces=PIECES,
    )
    msg = call(
        assemble_kernel, [], (), (swap(send, "core"),),
        into=[(msg, (ALL, slice(high, 2 * high)))],
    )
    got = exchange(msg, "far")
    pair = after(jnp.concatenate([node_feat, beside], axis=0), msg)
    pairs = [along_x(pair, k, nx) for k in range(1, nx)]
    dest = tile_dest.reshape(n)
    source = tile_source.reshape(n)
    order = hub_slots.reshape(far, 2, hub)
    order = jnp.where(core == 0, order, order[:, ::-1])
    order = jnp.swapaxes(order, 0, 1)
    slot_row, slot_col = order.reshape(1, slots), order.reshape(slots, 1)
    place, back, onehot, onehot_t, hub_t, feat_t, feat_self, degree = call(
        prepare_kernel,
        [
            shape((rows, n * tile), BF16),
            shape((panels, rows, per * tile), BF16),
            shape((rows, slots), BF16),
            shape((slots, rows), BF16),
            shape((rows, slots), BF16),
            square,
            square32,
            shape((rows, LANES), F32),
        ],
        (dest, source, core1, hub_source[0]),
        (
            tile_weights.reshape(n, tile, tile), after(node_feat, msg), slot_row, slot_col,
            hub_weights[0], self_weight,
        ),
        [pltpu.VMEM((slots, rows), BF16)], PREPARE_COST,
    )
    local = call(
        tiles_kernel, [square32], (source, here), (node_feat, beside, *pairs, place),
        [pltpu.VMEM((panels * rows, width), BF16), pltpu.VMEM((n * tile, width), BF16)],
        TILE_COST,
    )
    layer_out, dpre, gn, wkeep, wsend, packed, hsend = call(
        middle_kernel,
        [
            square, square, square, square32, square32,
            (shape((far, 2 * hub, width), BF16), (ALL, slice(0, hub))),
            shape((far, hub, width), BF16),
        ],
        (core1, me),
        (
            got, onehot, local, degree, feat_self, neigh_weight, cotangent, feat_t, onehot_t,
        ),
        [pltpu.VMEM((slots, width + 2 * LANES), BF16)],
    )
    deep = width * width // (2 * far * LANES)
    tiles = shape((2 * far, deep, LANES), F32)
    both = call(add_kernel, [tiles], (), (swap(wsend, "core"), wkeep))
    scattered = exchange(both, ("y", "far"))
    packed = call(
        assemble_kernel, [], (), (swap(after(hsend, both), "core"),),
        into=[(packed, (ALL, slice(hub, 2 * hub)))],
    )
    tall = 2 * rows + deep
    terms = call(
        panels_kernel,
        [shape((2 * rows, width), F32)]
        + [(shape((tall, width), BF16), (slice(0, 2 * rows),))] * (nx - 1),
        (dest, here), (after(gn, both), back), [pltpu.VMEM((per * tile, width), BF16)],
        PANEL_COST,
    )
    terms = [terms] if nx == 1 else terms
    scattered = after(scattered, (terms, packed))
    gathered = exchange(after(packed, scattered), "far")
    tail = (slice(2 * rows, tall),)
    part, *messages = as_list(
        call(
            sum_far_kernel, [shape((deep, LANES), F32)], (), (scattered,),
            into=[(x, tail) for x in terms[1:]],
        )
    )
    arrived = [along_x(messages[k - 1], k, nx) for k in range(1, nx)]
    total, panel_there, panel_here = call(
        sum_x_kernel, [tiles, square32, square32], (), (terms[0], part, *arrived)
    )
    total = after(total, gathered)
    panel_got = swap(after(panel_there, gathered), "y")
    mine = exchange(total, ("y", "far")).reshape(width // 8, width // LANES, 8, LANES)
    mine = jnp.swapaxes(mine, 1, 2).reshape(width, width)
    feat_grad = call(
        final_kernel, [square], (),
        (after(dpre, total), self_weight, hub_t, gathered, panel_here, panel_got),
        flops=FINAL_COST,
    )
    theirs = swap(after(mine, feat_grad), "core")
    self_grad = jnp.where(core == 0, mine, theirs)
    neigh_grad = jnp.where(core == 0, theirs, mine)
    return layer_out, feat_grad, self_grad, neigh_grad


def solution(mesh):
    nb, nd = mesh.devices.shape
    fine = Mesh(mesh.devices.reshape(2, nb // 2, nd // 2, 2), ("y", "x", "far", "core"))
    split = P(("y", "x", "far", "core"))
    in_specs = (split, split, P(), P(), split, split, split, split, split, split)
    out_specs = (split, split, P(), P())
    return jax.shard_map(
        per_device, mesh=fine, in_specs=in_specs, out_specs=out_specs, check_vma=False
    )
```

```python
import jax
import jax.numpy as jnp
from jax import lax
from jax.experimental import pallas as pl
from jax.experimental.pallas import tpu as pltpu
from jax.sharding import Mesh, PartitionSpec as P

F32 = jnp.float32
BF16 = jnp.bfloat16
LANES = 128
EXTRA = 8
PIECES = 2
SMALL = 1 << 10
TILE_COST = 1 << 10
PREPARE_COST = 22_000_000_000
PANEL_COST = 20_000_000_000
FINAL_COST = 20_000_000_000
NT = (((1,), (1,)), ((), ()))
NN = (((1,), (0,)), ((), ()))
ALL = slice(None)


def dot(a, b, dims=NN):
    return lax.dot_general(a, b, dims, preferred_element_type=F32)


def shape(dims, dtype):
    return jax.ShapeDtypeStruct(dims, dtype)


class Arrival:
    def __init__(self, copy, ref):
        self.copy, self.ref = copy, ref

    def __call__(self):
        if self.copy is not None:
            self.copy.wait()
            self.copy = None
        return self.ref


class Departure:
    def __init__(self, src, dst, sem):
        self.src, self.dst, self.sem = src, dst, sem
        self.ref, self.copies = src, []

    def send(self, piece=0, pieces=1):
        n = self.src.shape[0] // pieces
        rows = pl.ds(piece * n, n)
        copy = pltpu.make_async_copy(self.src.at[rows], self.dst.at[rows], self.sem.at[piece])
        copy.start()
        self.copies.append(copy)


def call(kernel, outs, scalars, arrays, scratch=(), flops=SMALL, into=(), pieces=1):
    def split(x):
        return x if isinstance(x, tuple) else (x, ())

    def window_shape(x, window):
        dims = list(x.shape)
        for i, part in enumerate(window):
            dims[i] = len(range(*part.indices(dims[i])))
        return pltpu.VMEM(tuple(dims), x.dtype)

    def cut(ref, window):
        return ref.at[window] if window else ref

    arrays, windows = zip(*[split(x) for x in arrays])
    outs = [split(x) for x in outs] + list(into)
    n_smem, n_in, n_out = len(scalars), len(arrays), len(outs)

    def body(*refs):
        smem, refs = refs[:n_smem], refs[n_smem:]
        src, refs = refs[:n_in], refs[n_in:]
        refs = refs[len(into) :]
        dst, refs = refs[:n_out], refs[n_out:]
        held, refs = refs[:n_in], refs[n_in:]
        made, refs = refs[:n_out], refs[n_out:]
        in_sem, out_sem, refs = refs[0], refs[1], refs[2:]
        ins = []
        for i in range(n_in):
            copy = pltpu.make_async_copy(cut(src[i], windows[i]), held[i], in_sem.at[i])
            copy.start()
            ins.append(Arrival(copy, held[i]))
        leaving = [
            Departure(made[i], cut(dst[i], outs[i][1]), out_sem.at[i]) for i in range(n_out)
        ]
        kernel(*smem, *ins, *leaving, *refs)
        for x in ins:
            x()
        for x in leaving:
            if not x.copies:
                x.send()
        for x in leaving:
            for copy in x.copies:
                copy.wait()

    smem = pl.BlockSpec(memory_space=pltpu.SMEM)
    hbm = pl.BlockSpec(memory_space=pltpu.MemorySpace.HBM)
    extra = [x for x, _ in into]
    first = n_out - len(into)
    result = pl.pallas_call(
        body,
        out_shape=[shape(x.shape, x.dtype) for x, _ in outs],
        in_specs=[smem] * n_smem + [hbm] * (n_in + len(extra)),
        out_specs=[hbm] * n_out,
        scratch_shapes=[window_shape(x, w) for x, w in zip(arrays, windows)]
        + [window_shape(x, w) for x, w in outs]
        + [pltpu.SemaphoreType.DMA((n_in,)), pltpu.SemaphoreType.DMA((n_out, pieces))]
        + list(scratch),
        input_output_aliases={n_smem + n_in + i: first + i for i in range(len(into))},
        cost_estimate=pl.CostEstimate(flops=flops, bytes_accessed=SMALL, transcendentals=0),
    )(*scalars, *arrays, *extra)
    return result if n_out > 1 else result[0]


def by_source(w, source, nblk):
    return [jnp.where(source == b, w, jnp.zeros_like(w)) for b in range(nblk)]


def hub_send_kernel(src, core, weights, feat, packed, send, wm_ref):
    w_ref = weights()
    owners, hub, tile = w_ref.shape
    per = LANES // hub
    flat = w_ref[...].reshape(owners * hub, tile)
    weight = dot(jnp.ones((EXTRA, tile), BF16), flat, NT)
    high = weight.astype(BF16).astype(F32)
    row = lax.broadcasted_iota(jnp.int32, weight.shape, 0)
    pair = jnp.where(row < EXTRA // 2, high, weight - high).astype(BF16)
    x_ref = feat()
    rows, width = x_ref.shape
    nblk = rows // tile
    top = (width // LANES) * hub
    n = owners // 2 // PIECES
    for message, other in ((send, 1 - core[0]), (packed, core[0])):
        msg_ref = message.ref
        for p in range(PIECES):
            for i in range(n):
                o = (p * n + i) * 2 + other
                for b, part in enumerate(by_source(w_ref[o], src[o], nblk)):
                    wm_ref[i * hub : (i + 1) * hub, b * tile : (b + 1) * tile] = part
            part = dot(wm_ref[...], x_ref[...]).astype(BF16)
            for c in range(width // LANES):
                msg_ref[p * n : (p + 1) * n, c * hub : (c + 1) * hub, :] = part[
                    :, c * LANES : (c + 1) * LANES
                ].reshape(n, hub, LANES)
            for i in range(p * n, (p + 1) * n):
                g = 2 * i // per
                msg_ref[i, top : top + EXTRA, :] = pair[:, g * LANES : (g + 1) * LANES]
            message.send(p, PIECES)


def prepare_kernel(
    dest, source, core, hub_source, tiles, feat, row, weights, self_weight,
    place, back, onehot, onehot_t, hub_t, feat_t, feat_self, degree, wm_ref,
):
    t_ref = tiles()
    place_ref, back_ref = place.ref, back.ref
    n, tile, _ = t_ref.shape
    rows = place_ref.shape[0]
    nblk = rows // tile
    per = back_ref.shape[2] // tile
    for i in range(n):
        t = t_ref[i]
        q, k = i // per, i % per
        d = dest[q, k]
        s = source[q, k]
        zero = jnp.zeros_like(t)
        tt = t.T
        for b in range(nblk):
            place_ref[b * tile : (b + 1) * tile, i * tile : (i + 1) * tile] = jnp.where(d == b, t, zero)
            keep = jnp.logical_and(s == b, d < nblk)
            back_ref[q, b * tile : (b + 1) * tile, k * tile : (k + 1) * tile] = jnp.where(keep, tt, zero)
    place.send()
    back.send()
    degree.ref[...] = dot(place_ref[...], jnp.ones((n * tile, LANES), BF16))
    degree.send()
    slots = onehot.ref.shape[1]
    r = lax.broadcasted_iota(jnp.int32, (rows, slots), 0)
    onehot.ref[...] = jnp.where(r == row()[...], 1.0, 0.0).astype(BF16)
    onehot.send()
    onehot_t.ref[...] = onehot.ref[...].T
    onehot_t.send()
    w_ref = weights()
    owners, hub, _ = w_ref.shape
    half = owners // 2
    for i in range(owners):
        o = (i % half) * 2 + (core[0] if i < half else 1 - core[0])
        for b, part in enumerate(by_source(w_ref[o], hub_source[o], nblk)):
            wm_ref[i * hub : (i + 1) * hub, b * tile : (b + 1) * tile] = part
    hub_t.ref[...] = wm_ref[...].T
    hub_t.send()
    x = feat()[...]
    feat_t.ref[...] = x.T
    feat_self.ref[...] = dot(x, self_weight()[...])


def tiles_kernel(source, here_y, here_x, own, beside, *rest):
    pairs, (place, out, halo_ref, rhs_ref) = rest[:-4], rest[-4:]
    tile = LANES
    rows = out.ref.shape[0]
    n = place.ref.shape[1] // tile
    nx = len(pairs) + 1
    per = n // (2 * nx)
    nblk = rows // tile
    halo_ref[:rows, :] = own()[...]
    halo_ref[rows : 2 * rows, :] = beside()[...]
    for i, pair in enumerate(pairs):
        halo_ref[2 * (i + 1) * rows : 2 * (i + 2) * rows, :] = pair()[...]
    for i in range(n):
        y, x = (i // per) // nx, (i // per) % nx
        back = lax.rem(here_x[0] - x + nx, nx)
        other = jnp.where(here_y[0] == y, 0, 1)
        at = pl.multiple_of(((back * 2 + other) * nblk + source[i // per, i % per]) * tile, tile)
        rhs_ref[i * tile : (i + 1) * tile, :] = halo_ref[pl.ds(at, tile), :]
    out.ref[...] = dot(place()[...], rhs_ref[...])


def middle_kernel(
    core, me, got, onehot, local, degree, feat_self, neigh_weight, cotangent, feat_t, onehot_t,
    layer_out, dpre_out, gn_out, wkeep, wsend, packed, hsend, rhs_ref,
):
    got_ref = got()
    far, both, _ = got_ref.shape
    rows, width = layer_out.ref.shape
    slots = onehot.ref.shape[1]
    half = slots // 2
    hub = half // far
    parts = width // LANES
    top = parts * hub
    slot = lax.broadcasted_iota(jnp.int32, (1, hub, LANES), 1)
    lane = lax.broadcasted_iota(jnp.int32, (1, hub, LANES), 2)
    mine = lane == lax.rem(me[0], LANES // hub) * hub + slot
    for r in range(2):
        at, base = slice(r * half, (r + 1) * half), r * (both // 2)
        for c in range(parts):
            rhs_ref[at, c * LANES : (c + 1) * LANES] = got_ref[
                :, base + c * hub : base + (c + 1) * hub, :
            ].reshape(half, LANES)
        for h in range(2):
            first = base + top + h * (EXTRA // 2)
            line = got_ref[:, first : first + 1, :].astype(F32)
            spread = jnp.where(mine, jnp.broadcast_to(line, (far, hub, LANES)), 0.0)
            rhs_ref[at, (parts + h) * LANES : (parts + h + 1) * LANES] = spread.astype(
                BF16
            ).reshape(half, LANES)
    hubs = dot(onehot()[...], rhs_ref[...])
    summed = local()[...] + hubs[:, :width]
    hub_deg = jnp.sum(
        hubs[:, width : width + LANES] + hubs[:, width + LANES : width + 2 * LANES],
        axis=1, keepdims=True,
    )
    scale = lax.rsqrt(degree()[:, :1] + hub_deg + 1.0)
    neigh = (summed * scale).astype(BF16)
    nw = neigh_weight()[...]
    pre = feat_self()[...] + dot(neigh, nw)
    sig = 1.0 / (1.0 + jnp.exp(-pre))
    dpre = (cotangent()[...].astype(F32) * (sig * (1.0 + pre * (1.0 - sig)))).astype(BF16)
    gn = (dot(dpre, nw, NT) * scale).astype(BF16)
    wself = dot(feat_t()[...], dpre)
    wneigh = dot(neigh.T, dpre)
    wsend.ref[...] = jnp.where(core[0] == 0, wneigh, wself)
    wsend.send()
    wkeep.ref[...] = jnp.where(core[0] == 0, wself, wneigh)
    wkeep.send()
    gn_out.ref[...] = gn
    gn_out.send()
    hot = onehot_t()
    hsend.ref[...] = dot(hot[slots // 2 :, :], gn).astype(BF16).reshape(hsend.ref.shape)
    hsend.send()
    packed.ref[...] = dot(hot[: slots // 2, :], gn).astype(BF16).reshape(packed.ref.shape)
    packed.send()
    layer_out.ref[...] = (pre * sig).astype(BF16)
    dpre_out.ref[...] = dpre


def add_kernel(got, keep, out):
    total = keep()[...] + got()[...]
    wide = total.shape[1] // LANES
    per = out.ref.shape[1] // 8
    for i in range(out.ref.shape[0] * per):
        r, c, k = i // wide, i % wide, i % per
        out.ref[i // per, 8 * k : 8 * (k + 1), :] = total[
            8 * r : 8 * (r + 1), c * LANES : (c + 1) * LANES
        ]


def assemble_kernel(got, out):
    out.ref[...] = got()[...]


def panels_kernel(dest, here_y, here_x, gn, back, *rest):
    outs, rhs_ref = rest[:-1], rest[-1]
    gn_ref, back_ref = gn(), back()
    panels, rows, depth = back_ref.shape
    tile = LANES
    per = depth // tile
    nblk = rows // tile
    nx = panels // 2
    for step in list(range(1, nx)) + [0]:
        out = outs[step]
        x = lax.rem(here_x[0] + step, nx)
        for other in range(2):
            q = (here_y[0] if other == 0 else 1 - here_y[0]) * nx + x
            for k in range(per):
                d = jnp.minimum(dest[q, k], nblk - 1)
                at = pl.multiple_of(d * tile, tile)
                rhs_ref[k * tile : (k + 1) * tile, :] = gn_ref[pl.ds(at, tile), :]
            part = dot(back_ref[q], rhs_ref[...])
            out.ref[other * rows : (other + 1) * rows, :] = part.astype(out.ref.dtype)
        out.send()


def sum_far_kernel(got, out, *rest):
    total = jnp.sum(got()[...], axis=0)
    high = total.astype(BF16)
    low = (total - high.astype(F32)).astype(BF16)
    for behind in rest:
        behind.ref[:, :LANES] = high
        behind.ref[:, LANES:] = low
        behind.send()
    out.ref[...] = total


def sum_x_kernel(own, part, *rest):
    messages, (tiles, there, here) = rest[:-3], rest[-3:]
    rows = here.ref.shape[0]
    small = part()[...]
    total = own()[...]
    for message in messages:
        ref = message()
        both = ref[2 * rows :, :].astype(F32)
        small = small + (both[:, :LANES] + both[:, LANES:])
        total = total + ref[: 2 * rows, :].astype(F32)
    tiles.ref[...] = jnp.broadcast_to(small[None], tiles.ref.shape)
    tiles.send()
    there.ref[...] = total[rows:]
    there.send()
    here.ref[...] = total[:rows]


def final_kernel(dpre, self_weight, hub_t, back, here, got, out):
    total = dot(dpre()[...], self_weight()[...], NT)
    back_ref, hub_ref = back(), hub_t()
    far, both, width = back_ref.shape
    hub = both // 2
    half = far * hub
    for i in range(2):
        rows = back_ref[:, i * hub : (i + 1) * hub, :].reshape(half, width)
        total = total + dot(hub_ref[:, i * half : (i + 1) * half], rows)
    out.ref[...] = (total + here()[...] + got()[...]).astype(BF16)


def as_list(x):
    return list(x) if isinstance(x, (list, tuple)) else [x]


def exchange(x, axis):
    return lax.all_to_all(x, axis, split_axis=0, concat_axis=0, tiled=True)


def swap(x, axis):
    return lax.ppermute(x, axis, [(0, 1), (1, 0)])


def along_x(x, step, nx):
    return lax.ppermute(x, "x", [(i, (i + step) % nx) for i in range(nx)])


def after(x, other):
    return lax.optimization_barrier((x, other))[0]


def per_device(
    node_feat, cotangent, self_weight, neigh_weight, tile_weights,
    tile_dest, tile_source, hub_weights, hub_source, hub_slots,
):
    rows, width = node_feat.shape
    _, panels, per, tile, _ = tile_weights.shape
    _, owners, hub, _ = hub_weights.shape
    n = panels * per
    slots = owners * hub
    high = (width // LANES) * hub + EXTRA
    far = lax.axis_size("far")
    nx = lax.axis_size("x")
    core = lax.axis_index("core").astype(jnp.int32)
    core1 = core.reshape(1)
    me = (lax.axis_index("far") * 2 + core).astype(jnp.int32).reshape(1)
    here = [lax.axis_index(name).astype(jnp.int32).reshape(1) for name in ("y", "x")]
    square = shape((rows, width), BF16)
    square32 = shape((rows, width), F32)
    beside = swap(node_feat, "y")
    msg, send = call(
        hub_send_kernel,
        [
            (shape((far, 2 * high, LANES), BF16), (ALL, slice(0, high))),
            shape((far, high, LANES), BF16),
        ],
        (hub_source[0], core1), (hub_weights[0], node_feat),
        [pltpu.VMEM((slots // 2 // PIECES, rows), BF16)], pieces=PIECES,
    )
    msg = call(
        assemble_kernel, [], (), (swap(send, "core"),),
        into=[(msg, (ALL, slice(high, 2 * high)))],
    )
    got = exchange(msg, "far")
    pair = after(jnp.concatenate([node_feat, beside], axis=0), msg)
    pairs = [along_x(pair, k, nx) for k in range(1, nx)]
    dest, source = tile_dest[0], tile_source[0]
    order = hub_slots.reshape(far, 2, hub)
    order = jnp.where(core == 0, order, order[:, ::-1])
    order = jnp.swapaxes(order, 0, 1)
    slot_row = order.reshape(1, slots)
    place, back, onehot, onehot_t, hub_t, feat_t, feat_self, degree = call(
        prepare_kernel,
        [
            shape((rows, n * tile), BF16),
            shape((panels, rows, per * tile), BF16),
            shape((rows, slots), BF16),
            shape((slots, rows), BF16),
            shape((rows, slots), BF16),
            square,
            square32,
            shape((rows, LANES), F32),
        ],
        (dest, source, core1, hub_source[0]),
        (
            tile_weights.reshape(n, tile, tile), after(node_feat, msg), slot_row,
            hub_weights[0], self_weight,
        ),
        [pltpu.VMEM((slots, rows), BF16)], PREPARE_COST,
    )
    local = call(
        tiles_kernel, [square32], (source, *here), (node_feat, beside, *pairs, place),
        [pltpu.VMEM((panels * rows, width), BF16), pltpu.VMEM((n * tile, width), BF16)],
        TILE_COST,
    )
    layer_out, dpre, gn, wkeep, wsend, packed, hsend = call(
        middle_kernel,
        [
            square, square, square, square32, square32,
            (shape((far, 2 * hub, width), BF16), (ALL, slice(0, hub))),
            shape((far, hub, width), BF16),
        ],
        (core1, me),
        (
            got, onehot, local, degree, feat_self, neigh_weight, cotangent, feat_t, onehot_t,
        ),
        [pltpu.VMEM((slots, width + 2 * LANES), BF16)],
    )
    deep = width * width // (2 * far * LANES)
    tiles = shape((2 * far, deep, LANES), F32)
    both = call(add_kernel, [tiles], (), (swap(wsend, "core"), wkeep))
    scattered = exchange(both, ("y", "far"))
    packed = call(
        assemble_kernel, [], (), (swap(after(hsend, both), "core"),),
        into=[(packed, (ALL, slice(hub, 2 * hub)))],
    )
    tall = 2 * rows + deep
    terms = call(
        panels_kernel,
        [shape((2 * rows, width), F32)]
        + [(shape((tall, width), BF16), (slice(0, 2 * rows),))] * (nx - 1),
        (dest, *here), (after(gn, both), back), [pltpu.VMEM((per * tile, width), BF16)],
        PANEL_COST,
    )
    terms = [terms] if nx == 1 else terms
    scattered = after(scattered, (terms, packed))
    gathered = exchange(after(packed, scattered), "far")
    tail = (slice(2 * rows, tall),)
    part, *messages = as_list(
        call(
            sum_far_kernel, [shape((deep, LANES), F32)], (), (scattered,),
            into=[(x, tail) for x in terms[1:]],
        )
    )
    arrived = [along_x(messages[k - 1], k, nx) for k in range(1, nx)]
    total, panel_there, panel_here = call(
        sum_x_kernel, [tiles, square32, square32], (), (terms[0], part, *arrived)
    )
    total = after(total, gathered)
    panel_got = swap(after(panel_there, gathered), "y")
    mine = exchange(total, ("y", "far")).reshape(width // 8, width // LANES, 8, LANES)
    mine = jnp.swapaxes(mine, 1, 2).reshape(width, width)
    feat_grad = call(
        final_kernel, [square], (),
        (after(dpre, total), self_weight, hub_t, gathered, panel_here, panel_got),
        flops=FINAL_COST,
    )
    theirs = swap(after(mine, feat_grad), "core")
    self_grad = jnp.where(core == 0, mine, theirs)
    neigh_grad = jnp.where(core == 0, theirs, mine)
    return layer_out, feat_grad, self_grad, neigh_grad


def solution(mesh):
    nb, nd = mesh.devices.shape
    fine = Mesh(mesh.devices.reshape(2, nb // 2, nd // 2, 2), ("y", "x", "far", "core"))
    split = P(("y", "x", "far", "core"))
    in_specs = (split, split, P(), P(), split, split, split, split, split, split)
    out_specs = (split, split, P(), P())
    return jax.shard_map(
        per_device, mesh=fine, in_specs=in_specs, out_specs=out_specs, check_vma=False
    )
```
